256 devices in a mesh: replica: 8 (over x, core), outer: 4 (over y), link: 8 (over z).
Axes of the slice: x: 4, y: 4, z: 8, core: 2. Of those that a mesh axis runs over, the one named last changes fastest.
Arguments:
- link_in: bfloat16 [8, 16384, 256], P('replica', ('outer', 'link')), may hold values from -6 to 6
- path_in: bfloat16 [8, 4096, 256], P('replica', ('outer', 'link')), may hold values from -6 to 6
- hop_slots: int32 [8, 4096, 24], P('replica', ('outer', 'link')), may hold values from 0 to 2047
- hop_lens: int32 [8, 4096], P('replica', ('outer', 'link')), may hold values from 2 to 24
- failed: int32 [8, 16384], P('replica', ('outer', 'link')), may hold values 0 or 1
- serve_index: int32 [8, 32, 32, 64], P('replica', None, ('outer', 'link')), may hold values from 0 to 511
- link_grad: bfloat16 [8, 16384, 256], P('replica', ('outer', 'link')), may hold values from -6 to 6
- path_grad: bfloat16 [8, 4096, 256], P('replica', ('outer', 'link')), may hold values from -6 to 6
- gru_wx: bfloat16 [256, 768], replicated, may hold values from -0.375 to 0.375
- gru_wh: bfloat16 [256, 768], replicated, may hold values from -0.375 to 0.375
- gru_bias: float32 [768], replicated, may hold values from -3 to 3
- mlp_w1: bfloat16 [512, 256], replicated, may hold values from -0.25 to 0.25
- mlp_b1: float32 [256], replicated, may hold values from -3 to 3
- mlp_w2: bfloat16 [256, 256], replicated, may hold values from -0.375 to 0.375
- mlp_b2: float32 [256], replicated, may hold values from -3 to 3
Outputs:
- link_out: bfloat16 [8, 16384, 256], P('replica', ('outer', 'link'))
- path_out: bfloat16 [8, 4096, 256], P('replica', ('outer', 'link'))
- link_in_grad: float32 [8, 16384, 256], P('replica', ('outer', 'link'))
- path_in_grad: float32 [8, 4096, 256], P('replica', ('outer', 'link'))
- grad_wx: float32 [256, 768], replicated
- grad_wh: float32 [256, 768], replicated
- grad_bias: float32 [768], replicated
- grad_w1: float32 [512, 256], replicated
- grad_b1: float32 [256], replicated
- grad_w2: float32 [256, 256], replicated
- grad_b2: float32 [256], replicated
The draws below stay inside these ranges and needn't reach their ends.
Inputs may be any that keep to these rules, and one draw needn't show every extreme that they name: `serve_index`: entry [s, d, o, c] names, among the 512 links of owner device o, the link in request slot c of device d; a link may fill several slots. `hop_slots`: slot o * 64 + c is request slot c of the flow's own device towards owner o; entries at hops past the flow's length are ignored. 1 marks a failed link.
All inputs are finite; a program needn't handle non-finite values. No bound on the sum of `failed` on one device may be relied on, other than what follows from the above.
Results may differ from the reference program's by a relative error of at most 0.0067.
Values may be sent and summed in bfloat16 or wider, within the bound.
No kernel may reach another device: no remote copies, remote signals or barrier semaphores. Data moves between devices by JAX's collectives and lax.ppermute only.
A program may use at most 128 MiB of HBM per device.

```python
import math
import jax
import jax.numpy as jnp
import numpy as np
from jax import lax

D = 256
H = 24
F_DEV = 128
L_DEV = 512
GROUP = 32
CAP = 64
SCEN = 8
LINKS = 16384
FLOWS = 4096


def place_ends(drawn, rng, low, largest):
    place = [jax.random.randint(jax.random.fold_in(rng, axis), (), 0, length) for axis, length in enumerate(drawn.shape)]
    longest = drawn.shape.index(max(drawn.shape))
    next_to = place[:longest] + [(place[longest] + 1) % drawn.shape[longest]] + place[longest + 1:]
    return drawn.at[tuple(place)].set(low).at[tuple(next_to)].set(largest)


def levels(stream_key, extent, cuts, smallest, largest):
    gain = 1.0
    for dim, shards_of in cuts:
        draws = jax.random.uniform(jax.random.fold_in(jax.random.fold_in(stream_key, 6), dim), (shards_of,), jnp.float32, smallest / len(cuts), largest / len(cuts))
        gain = gain * jnp.repeat(jnp.exp(draws), extent[dim] // shards_of).reshape((-1,) + (1,) * (len(extent) - 1 - dim))
    return gain


def rank_table(count, slope):
    weights = [(1 << 20) // math.isqrt(standing ** slope) + 1 for standing in range(1, count + 1)]
    spread = 1 + sum(weights) // (1 << 30)
    return np.cumsum(np.array([max(1, weight // spread) for weight in weights]))


def skewed_ids(rng, dims, amount, skew):
    listing = rank_table(amount, skew)
    lot = jax.random.randint(jax.random.fold_in(rng, 1), dims, 0, int(listing[amount - 1]))
    rank = jnp.searchsorted(jnp.asarray(listing, jnp.int32), lot, side="right")
    return jax.random.permutation(jax.random.fold_in(rng, 2), amount)[rank].astype(jnp.int32)


def noise(stream_key, dims, spread, bound, pieces=(), held_as=jnp.bfloat16):
    loudness = levels(stream_key, dims, pieces, -0.22, 0.18) if pieces else 1.0
    values = jax.random.normal(stream_key, dims, jnp.float32) * spread * loudness
    return jnp.minimum(jnp.maximum(values, -bound), bound).astype(held_as)


def setup_inputs(seed: int = 0) -> dict:
    key_of = jax.random.split(jax.random.key(seed), 16)
    link_in = noise(key_of[0], (SCEN, LINKS, D), 1.0, 6.0, ((0, 8), (1, 32)))
    path_in = noise(key_of[1], (SCEN, FLOWS, D), 1.0, 6.0, ((0, 8), (1, 32)))
    hop_slots = place_ends(skewed_ids(key_of[2], (SCEN, FLOWS, H), GROUP * CAP, 1), jax.random.fold_in(key_of[2], 3), 0, (GROUP * CAP) - 1).astype(jnp.int32)
    hop_lens = place_ends(jax.random.randint(key_of[3], (SCEN, FLOWS), 2, H + 1), jax.random.fold_in(key_of[3], 1), 2, H).astype(jnp.int32)
    failed = place_ends((jax.random.randint(key_of[4], (SCEN, LINKS), 0, 16) < 1).astype(jnp.int32), jax.random.fold_in(key_of[4], 1), 0, 1)
    serve_index = place_ends(jax.random.randint(key_of[5], (SCEN, GROUP, GROUP, CAP), 0, L_DEV), jax.random.fold_in(key_of[5], 1), 0, L_DEV - 1).astype(jnp.int32)
    link_grad = noise(key_of[6], (SCEN, LINKS, D), 1.0, 6.0, ((0, 8), (1, 32)))
    path_grad = noise(key_of[7], (SCEN, FLOWS, D), 1.0, 6.0, ((0, 8), (1, 32)))
    gru_wx = noise(key_of[8], (D, 3 * D), D ** -0.5, 0.375)
    gru_wh = noise(key_of[9], (D, 3 * D), D ** -0.5, 0.375)
    gru_bias = noise(key_of[10], (3 * D,), 0.5, 3.0, (), jnp.float32)
    mlp_w1 = noise(key_of[11], (2 * D, D), (2 * D) ** -0.5, 0.25)
    mlp_b1 = noise(key_of[12], (D,), 0.5, 3.0, (), jnp.float32)
    mlp_w2 = noise(key_of[13], (D, D), D ** -0.5, 0.375)
    mlp_b2 = noise(key_of[14], (D,), 0.5, 3.0, (), jnp.float32)
    return {"link_in": link_in, "path_in": path_in, "hop_slots": hop_slots, "hop_lens": hop_lens, "failed": failed, "serve_index": serve_index, "link_grad": link_grad, "path_grad": path_grad, "gru_wx": gru_wx, "gru_wh": gru_wh, "gru_bias": gru_bias, "mlp_w1": mlp_w1, "mlp_b1": mlp_b1, "mlp_w2": mlp_w2, "mlp_b2": mlp_b2}


def gate_terms(state_now, hop_input, input_weight, hidden_weight, gate_bias):
    from_input = jnp.dot(hop_input, input_weight, preferred_element_type=jnp.float32) + gate_bias
    from_state = jnp.dot(state_now.astype(jnp.bfloat16), hidden_weight, preferred_element_type=jnp.float32)
    return from_input, from_state


def gru_cell(state_now, from_input, from_state):
    feat_width = state_now.shape[1]
    update = jax.nn.sigmoid(from_input[:, :feat_width] + from_state[:, :feat_width])
    reset = jax.nn.sigmoid(from_input[:, feat_width:2 * feat_width] + from_state[:, feat_width:2 * feat_width])
    candidate = jnp.tanh(from_input[:, 2 * feat_width:] + reset * from_state[:, 2 * feat_width:])
    return candidate + update * (state_now - candidate), update, reset, candidate


def gru_forward(path_start, hop_inputs, live_mask, input_weight, hidden_weight, gate_bias, keep_gates):
    def advance(state_now, scan_item):
        hop_input, live_now = scan_item
        from_input, from_state = gate_terms(state_now, hop_input, input_weight, hidden_weight, gate_bias)
        stepped = gru_cell(state_now, from_input, from_state)[0]
        state_next = jnp.where(live_now[:, None] > 0, stepped, state_now)
        if keep_gates:
            return state_next, (state_next, from_input, from_state)
        return state_next, (state_next,)
    return lax.scan(advance, path_start.astype(jnp.float32), (hop_inputs, live_mask))[1]


def back_step(carried, hop_input, state_now, live_now, hop_grad, from_input, from_state, input_tr, hidden_tr):
    grad_state, grad_wx, grad_wh, grad_bias = carried
    feat_width = state_now.shape[1]
    live_col = live_now[:, None]
    grad_state = grad_state + live_col * hop_grad
    update, reset, candidate = gru_cell(state_now, from_input, from_state)[1:]
    pre_update = grad_state * (state_now - candidate) * update * (1.0 - update)
    pre_cand = grad_state * (1.0 - update) * (1.0 - candidate * candidate)
    pre_reset = pre_cand * from_state[:, 2 * feat_width:] * reset * (1.0 - reset)
    grad_in = jnp.concatenate([pre_update, pre_reset, pre_cand], axis=1) * live_col
    grad_hid = jnp.concatenate([pre_update, pre_reset, pre_cand * reset], axis=1) * live_col
    in_bf = grad_in.astype(jnp.bfloat16)
    hid_bf = grad_hid.astype(jnp.bfloat16)
    grad_prev = jnp.where(live_col > 0, grad_state * update + jnp.dot(hid_bf, hidden_tr, preferred_element_type=jnp.float32), grad_state)
    grad_input = jnp.dot(in_bf, input_tr, preferred_element_type=jnp.float32)
    grad_wx = grad_wx + jnp.dot(hop_input.T, in_bf, preferred_element_type=jnp.float32)
    grad_wh = grad_wh + jnp.dot(state_now.astype(jnp.bfloat16).T, hid_bf, preferred_element_type=jnp.float32)
    grad_bias = grad_bias + jnp.sum(grad_in, axis=0)
    return (grad_prev, grad_wx, grad_wh, grad_bias), grad_input


def gru_backward(path_start, states, hop_inputs, live_mask, hop_grads, path_grad, input_weight, hidden_weight, gate_bias, kept):
    feat_width = path_start.shape[1]
    prior_states = jnp.concatenate([path_start.astype(jnp.float32)[None], states[:-1]], axis=0)
    input_tr = input_weight.T
    hidden_tr = hidden_weight.T
    initial = (path_grad.astype(jnp.float32), jnp.zeros((feat_width, 3 * feat_width), jnp.float32),
               jnp.zeros((feat_width, 3 * feat_width), jnp.float32), jnp.zeros((3 * feat_width,), jnp.float32))
    if kept is None:
        def retreat(carried, scan_item):
            hop_input, state_now, live_now, hop_grad = scan_item
            from_input, from_state = gate_terms(state_now, hop_input, input_weight, hidden_weight, gate_bias)
            return back_step(carried, hop_input, state_now, live_now, hop_grad, from_input, from_state, input_tr, hidden_tr)
        scan_items = (hop_inputs, prior_states, live_mask, hop_grads)
    else:
        def retreat(carried, scan_item):
            hop_input, state_now, live_now, hop_grad, from_input, from_state = scan_item
            return back_step(carried, hop_input, state_now, live_now, hop_grad, from_input, from_state, input_tr, hidden_tr)
        scan_items = (hop_inputs, prior_states, live_mask, hop_grads, kept[0], kept[1])
    return lax.scan(retreat, initial, scan_items, reverse=True)


def link_forward(link_rows, agg_bf, keep_col, mlp_w1, mlp_b1, mlp_w2, mlp_b2):
    feat_width = link_rows.shape[1]
    pre_act = (jnp.dot(link_rows, mlp_w1[:feat_width], preferred_element_type=jnp.float32)
               + jnp.dot(agg_bf, mlp_w1[feat_width:], preferred_element_type=jnp.float32) + mlp_b1)
    activ = jax.nn.silu(pre_act).astype(jnp.bfloat16)
    value = link_rows.astype(jnp.float32) + jnp.dot(activ, mlp_w2, preferred_element_type=jnp.float32) + mlp_b2
    return (keep_col * value).astype(jnp.bfloat16), pre_act, activ


def link_backward(link_grad_rows, link_rows, agg_bf, keep_col, pre_act, activ, mlp_w1, mlp_w2):
    feat_width = link_rows.shape[1]
    grad_val = keep_col * link_grad_rows.astype(jnp.float32)
    val_bf = grad_val.astype(jnp.bfloat16)
    grad_w2 = jnp.dot(activ.T, val_bf, preferred_element_type=jnp.float32)
    grad_b2 = jnp.sum(grad_val, axis=0)
    grad_act = jnp.dot(val_bf, mlp_w2.T, preferred_element_type=jnp.float32)
    sigma = jax.nn.sigmoid(pre_act)
    grad_pre = grad_act * sigma * (1.0 + pre_act * (1.0 - sigma))
    pre_bf = grad_pre.astype(jnp.bfloat16)
    grad_w1 = jnp.concatenate([jnp.dot(link_rows.T, pre_bf, preferred_element_type=jnp.float32),
                               jnp.dot(agg_bf.T, pre_bf, preferred_element_type=jnp.float32)], axis=0)
    grad_b1 = jnp.sum(grad_pre, axis=0)
    link_direct = grad_val + jnp.dot(pre_bf, mlp_w1[:feat_width].T, preferred_element_type=jnp.float32)
    agg_grad = jnp.dot(pre_bf, mlp_w1[feat_width:].T, preferred_element_type=jnp.float32).astype(jnp.bfloat16)
    return link_direct, agg_grad, (grad_w1, grad_b1, grad_w2, grad_b2)


def reference(link_in, path_in, hop_slots, hop_lens, failed, serve_index, link_grad, path_grad, gru_wx, gru_wh, gru_bias, mlp_w1, mlp_b1, mlp_w2, mlp_b2):
    slot_count = GROUP * CAP
    owner_base = (jnp.arange(GROUP, dtype=jnp.int32) * L_DEV)[None, :, None]
    hop_range = jnp.arange(H, dtype=jnp.int32)
    flow_device = jnp.arange(FLOWS, dtype=jnp.int32) // F_DEV

    def scenario(carried, scan_item):
        links_s, paths_s, slots_s, lens_s, failed_s, serve_s, lgrad_s, pgrad_s = scan_item
        glink = (serve_s + owner_base).reshape(GROUP * slot_count).astype(jnp.int32)
        key_rows = (flow_device[:, None] * slot_count + slots_s).T.astype(jnp.int32)
        link_ids = glink[key_rows]
        live_mask = (hop_range[:, None] < lens_s[None, :]).astype(jnp.float32)
        hop_inputs = links_s[link_ids]
        states, from_inputs, from_states = gru_forward(paths_s, hop_inputs, live_mask, gru_wx, gru_wh, gru_bias, True)
        partial_value = jax.ops.segment_sum((states * live_mask[:, :, None]).reshape(H * FLOWS, D), key_rows.reshape(-1),
                                      num_segments=GROUP * slot_count).astype(jnp.bfloat16)
        aggregate = jax.ops.segment_sum(partial_value.astype(jnp.float32), glink, num_segments=LINKS)
        agg_bf = aggregate.astype(jnp.bfloat16)
        keep_col = (1 - failed_s).astype(jnp.float32)[:, None]
        link_out, pre_act, activ = link_forward(links_s, agg_bf, keep_col, mlp_w1, mlp_b1, mlp_w2, mlp_b2)
        path_out = states[-1].astype(jnp.bfloat16)
        link_direct, agg_grad, mlp_terms = link_backward(lgrad_s, links_s, agg_bf, keep_col, pre_act, activ, mlp_w1, mlp_w2)
        hop_grads = agg_grad[link_ids].astype(jnp.float32) * live_mask[:, :, None]
        finished, grad_inputs = gru_backward(paths_s, states, hop_inputs, live_mask, hop_grads, pgrad_s,
                                             gru_wx, gru_wh, gru_bias, (from_inputs, from_states))
        dpart = jax.ops.segment_sum(grad_inputs.reshape(H * FLOWS, D), key_rows.reshape(-1),
                                    num_segments=GROUP * slot_count).astype(jnp.bfloat16)
        link_back = link_direct + jax.ops.segment_sum(dpart.astype(jnp.float32), glink, num_segments=LINKS)
        terms = (finished[1], finished[2], finished[3]) + mlp_terms
        summed = tuple(total + term for total, term in zip(carried, terms))
        return summed, (link_out, path_out, link_back, finished[0])

    zero_grads = (jnp.zeros((D, 3 * D), jnp.float32), jnp.zeros((D, 3 * D), jnp.float32), jnp.zeros((3 * D,), jnp.float32),
                  jnp.zeros((2 * D, D), jnp.float32), jnp.zeros((D,), jnp.float32), jnp.zeros((D, D), jnp.float32),
                  jnp.zeros((D,), jnp.float32))
    grads, (link_out, path_out, link_back, path_back) = lax.scan(
        scenario, zero_grads, (link_in, path_in, hop_slots, hop_lens, failed, serve_index, link_grad, path_grad))
    grad_scale = float(SCEN * LINKS) ** -0.5
    return (link_out, path_out, link_back, path_back, grads[0] * grad_scale, grads[1] * grad_scale, grads[2] * grad_scale,
            grads[3] * grad_scale, grads[4] * grad_scale, grads[5] * grad_scale, grads[6] * grad_scale)
```

```python
import jax
import jax.numpy as jnp
from jax import lax
from jax.experimental import pallas as pl
from jax.experimental.pallas import tpu as pltpu
from jax.sharding import PartitionSpec as P

F32 = jnp.float32
BF = jnp.bfloat16
INTERPRET = False
OL = ("outer", "link")


def dot(a, b):
    return jnp.dot(a, b, preferred_element_type=F32)


def dot_nt(a, b):
    return lax.dot_general(a, b, (((1,), (1,)), ((), ())), preferred_element_type=F32)


def dot_tn(a, b):
    return lax.dot_general(a, b, (((0,), (0,)), ((), ())), preferred_element_type=F32)


def sigmoid(v):
    return 0.5 * jnp.tanh(0.5 * v) + 0.5


def pick_cols(col, width):
    lanes = lax.broadcasted_iota(jnp.int32, (col.shape[0], width), 1)
    return jnp.where(lanes == col, 1.0, 0.0).astype(BF)


def pick_rows(row, height, base=0):
    subs = lax.broadcasted_iota(jnp.int32, (height, row.shape[1]), 0) + base
    return jnp.where(subs == row, 1.0, 0.0).astype(BF)


def call(kernel, outs, **kw):
    return pl.pallas_call(kernel, out_shape=outs, interpret=INTERPRET, **kw)


def sds(shape, dtype):
    return jax.ShapeDtypeStruct(shape, dtype)


def gather_rows(table, serve_col, out_ref, per=8):
    cap, group = serve_col.shape
    links = table.shape[0]
    for o in range(0, group, per):
        sel = jnp.concatenate(
            [pick_cols(serve_col[:, k : k + 1], links) for k in range(o, o + per)], axis=0
        )
        out_ref[o * cap : (o + per) * cap, :] = dot(sel, table).astype(BF)


def serve_kernel(table_ref, col_ref, out_ref):
    gather_rows(table_ref[...], col_ref[...], out_ref)


def fetch_hops(table_ref, slot_ref, out_ref, per=4):
    flows, hops = slot_ref.shape
    slots = table_ref.shape[0]
    table = table_ref[...]
    cols = slot_ref[...]
    for t in range(0, hops, per):
        sel = jnp.concatenate(
            [pick_cols(cols[:, k : k + 1], slots) for k in range(t, t + per)], axis=0
        )
        rows = dot(sel, table).astype(out_ref.dtype)
        for k in range(per):
            out_ref[t + k] = rows[k * flows : (k + 1) * flows]


def sum_slots(row_ref, rows, out_ref, block=512):
    hops = row_ref.shape[0]
    slots = out_ref.shape[0]
    idx = row_ref[...]
    for q in range(0, slots, block):
        sel = jnp.concatenate([pick_rows(idx[t : t + 1, :], block, q) for t in range(hops)], axis=1)
        out_ref[q : q + block, :] = dot(sel, rows).astype(BF)


def forward_kernel(
    table_ref, slot_ref, row_ref, lens_ref, path_ref, wx_ref, wh_ref, bias_ref,
    x_ref, state_ref, part_ref, pathout_ref, gi_ref, hb_ref,
):
    hops, flows, width = x_ref.shape
    fetch_hops(table_ref, slot_ref, x_ref)
    per = 4
    for t in range(0, hops, per):
        rows = x_ref[t : t + per].reshape(per * flows, width)
        gi = dot(rows, wx_ref[...]) + bias_ref[...]
        gi_ref[t : t + per] = gi.reshape(per, flows, 3 * width)
    lens = lens_ref[...]

    def step(t, h):
        state_ref[t] = h
        gs = dot(h.astype(BF), wh_ref[...])
        gi = gi_ref[t]
        z = sigmoid(gi[:, :width] + gs[:, :width])
        r = sigmoid(gi[:, width : 2 * width] + gs[:, width : 2 * width])
        n = jnp.tanh(gi[:, 2 * width :] + r * gs[:, 2 * width :])
        h = jnp.where(t < lens, n + z * (h - n), h)
        hb_ref[t] = h.astype(BF)
        return h

    h = lax.fori_loop(0, hops, step, path_ref[...].astype(F32), unroll=2)
    pathout_ref[...] = h.astype(BF)
    sum_slots(row_ref, hb_ref[...].reshape(hops * flows, width), part_ref)


def coef_kernel(x_ref, state_ref, lens_ref, wx_ref, wh_ref, bias_ref, coef_ref):
    per, flows, width = x_ref.shape
    first = pl.program_id(0) * per
    rows = x_ref[...].reshape(per * flows, width)
    gi = dot(rows, wx_ref[...]) + bias_ref[...]
    h = state_ref[...].reshape(per * flows, width)
    gs = dot(h.astype(BF), wh_ref[...])
    z = sigmoid(gi[:, :width] + gs[:, :width])
    r = sigmoid(gi[:, width : 2 * width] + gs[:, width : 2 * width])
    gs3 = gs[:, 2 * width :]
    n = jnp.tanh(gi[:, 2 * width :] + r * gs3)
    cz = (h - n) * z * (1.0 - z)
    cn = (1.0 - z) * (1.0 - n * n)
    cr = cn * gs3 * r * (1.0 - r)
    for k in range(per):
        live = (first + k) < lens_ref[...]
        s = slice(k * flows, (k + 1) * flows)
        coef_ref[k, 0] = jnp.where(live, z[s], 1.0)
        coef_ref[k, 1] = jnp.where(live, cz[s], 0.0)
        coef_ref[k, 2] = jnp.where(live, cr[s], 0.0)
        coef_ref[k, 3] = jnp.where(live, cn[s], 0.0)
        coef_ref[k, 4] = r[s]


def link_kernel(
    got_ref, srow_ref, scol_ref, link_ref, lgrad_ref, keep_ref, w1_ref, b1_ref, w2_ref,
    out_ref, agg_ref, act_ref, du_ref, db1_ref,
):
    links, width = link_ref.shape
    sel = jnp.concatenate(
        [pick_rows(srow_ref[k : k + 1, :], links) for k in range(srow_ref.shape[0])], axis=1
    )
    agg = dot(sel, got_ref[...]).astype(BF)
    agg_ref[...] = agg
    u = dot(link_ref[...], w1_ref[:width, :]) + dot(agg, w1_ref[width:, :]) + b1_ref[...]
    s = sigmoid(u)
    act_ref[...] = (u * s).astype(BF)
    gv = (keep_ref[...] * lgrad_ref[...].astype(F32)).astype(BF)
    du = dot_nt(gv, w2_ref[...]) * s * (1.0 + u * (1.0 - s))
    db1_ref[...] = jnp.sum(du, axis=0, keepdims=True)
    du = du.astype(BF)
    du_ref[...] = du
    dagg = dot_nt(du, w1_ref[width:, :]).astype(BF)
    gather_rows(dagg, scol_ref[...], out_ref)


def link_rest_kernel(
    link_ref, lgrad_ref, keep_ref, agg_ref, act_ref, du_ref, db1_ref, w1_ref, w2_ref, b2_ref,
    lout_ref, direct_ref, pack_ref,
):
    _, width = link_ref.shape
    link = link_ref[...]
    keep = keep_ref[...]
    act = act_ref[...]
    du = du_ref[...]
    value = link.astype(F32) + dot(act, w2_ref[...]) + b2_ref[...]
    lout_ref[...] = (keep * value).astype(BF)
    gv = keep * lgrad_ref[...].astype(F32)
    direct_ref[...] = gv + dot_nt(du, w1_ref[:width, :])
    pack_ref[0:width, :] = dot_tn(link, du).astype(BF)
    pack_ref[width : 2 * width, :] = dot_tn(agg_ref[...], du).astype(BF)
    pack_ref[2 * width : 3 * width, :] = dot_tn(act, gv.astype(BF)).astype(BF)
    db2 = jnp.sum(gv, axis=0, keepdims=True)
    tail = jnp.concatenate([db1_ref[...], db2, jnp.zeros((14, width), F32)], axis=0)
    pack_ref[3 * width :, :] = tail.astype(BF)


def backward_kernel(
    table_ref, slot_ref, row_ref, pgrad_ref, wx_ref, wh_ref, coef_hbm,
    part_ref, pathgrad_ref, dgi_ref, dgs_ref, db_ref,
    hg_ref, coef_ref, dx_ref, sem,
):
    hops, flows, width = hg_ref.shape

    def load(t):
        return pltpu.make_async_copy(coef_hbm.at[t], coef_ref.at[t], sem.at[t])

    for t in range(hops - 1, -1, -1):
        load(t).start()
    fetch_hops(table_ref, slot_ref, hg_ref)
    db_ref[...] = jnp.zeros(db_ref.shape, F32)

    def fold(v):
        return jnp.sum(v.reshape(flows // 8, 8, width), axis=0)

    def step(k, g):
        t = hops - 1 - k
        load(t).wait()
        g = g + hg_ref[t].astype(F32)
        az = g * coef_ref[t, 1]
        ar = g * coef_ref[t, 2]
        an = g * coef_ref[t, 3]
        azb = az.astype(BF)
        arb = ar.astype(BF)
        anr = (an * coef_ref[t, 4]).astype(BF)
        dgs = jnp.concatenate([azb, arb, anr], axis=1)
        nxt = g * coef_ref[t, 0] + dot_nt(dgs, wh_ref[...])
        dgs_ref[t] = dgs
        dgi_ref[t] = jnp.concatenate([azb, arb, an.astype(BF)], axis=1)
        db_ref[:, :width] += fold(az)
        db_ref[:, width : 2 * width] += fold(ar)
        db_ref[:, 2 * width :] += fold(an)
        return nxt

    g = lax.fori_loop(0, hops, step, pgrad_ref[...].astype(F32), unroll=2)
    pathgrad_ref[...] = g
    per = 4
    for t in range(0, hops, per):
        rows = dgi_ref[t : t + per].reshape(per * flows, 3 * width)
        dx_ref[t * flows : (t + per) * flows, :] = dot_nt(rows, wx_ref[...]).astype(BF)
    sum_slots(row_ref, dx_ref[...], part_ref)


def weight_kernel(x_ref, state_ref, dgi_ref, dgs_ref, db_ref, mlp_ref, pack_ref, awx_ref, awh_ref):
    per, flows, width = x_ref.shape
    i = pl.program_id(0)
    x = x_ref[...].reshape(per * flows, width)
    h = state_ref[...].reshape(per * flows, width).astype(BF)
    gx = dot_tn(x, dgi_ref[...].reshape(per * flows, 3 * width))
    gh = dot_tn(h, dgs_ref[...].reshape(per * flows, 3 * width))

    @pl.when(i == 0)
    def _():
        awx_ref[...] = gx
        awh_ref[...] = gh

    @pl.when(i > 0)
    def _():
        awx_ref[...] += gx
        awh_ref[...] += gh

    @pl.when(i == pl.num_programs(0) - 1)
    def _():
        for k in range(3):
            s = slice(k * width, (k + 1) * width)
            pack_ref[k * width : (k + 1) * width, :] = awx_ref[:, s].astype(BF)
            pack_ref[(3 + k) * width : (4 + k) * width, :] = awh_ref[:, s].astype(BF)
        base = 9 * width
        pack_ref[6 * width : base + 16, :] = mlp_ref[...]
        b = jnp.sum(db_ref[...], axis=0, keepdims=True)
        tail = jnp.concatenate(
            [b[:, k * width : (k + 1) * width] for k in range(3)] + [jnp.zeros((13, width), F32)],
            axis=0,
        )
        pack_ref[base + 16 : base + 32, :] = tail.astype(BF)
        rest = pack_ref.shape[0] - base - 32
        pack_ref[base + 32 :, :] = jnp.zeros((rest, width), BF)


def finish_kernel(got_ref, srow_ref, direct_ref, out_ref):
    links = direct_ref.shape[0]
    sel = jnp.concatenate(
        [pick_rows(srow_ref[k : k + 1, :], links) for k in range(srow_ref.shape[0])], axis=1
    )
    out_ref[...] = direct_ref[...] + dot(sel, got_ref[...])


def swap(blocks, axes=OL, groups=None):
    return lax.all_to_all(
        blocks, axes, split_axis=0, concat_axis=0, tiled=True, axis_index_groups=groups
    )


def swap_named(rows, group):
    return swap(rows.reshape(group, -1, rows.shape[1])).reshape(rows.shape)


def total(v):
    return jnp.sum(v.astype(F32), axis=0).astype(BF)


def pair_kernel(place_ref, pack_ref, got_ref, *out_refs):
    x = place_ref[0]
    core = place_ref[1]
    chips = got_ref.shape[0]
    for k in range(chips):
        c = lax.rem(x + k, chips)
        both = pack_ref[core * chips + c].astype(F32) + got_ref[c].astype(F32)
        out_refs[k][...] = both.astype(BF)


def unpack_kernel(place_ref, *refs, scale):
    x = place_ref[0]
    core = place_ref[1]
    chips = (len(refs) - 8) // 2
    mine = refs[:chips]
    got = refs[chips : 2 * chips]
    wx_ref, wh_ref, bias_ref, w1_ref, b1_ref, w2_ref, b2_ref, all_ref = refs[2 * chips :]
    rows, width = mine[0].shape
    for k in range(chips):
        c = lax.rem(x - k + chips, chips)
        all_ref[pl.ds(pl.multiple_of((core * chips + c) * rows, 64), rows), :] = mine[k][...]
        all_ref[pl.ds(pl.multiple_of(((1 - core) * chips + c) * rows, 64), rows), :] = got[k][...]
    take = lambda a, n: all_ref[a : a + n, :].astype(F32) * scale
    for k in range(3):
        s = slice(k * width, (k + 1) * width)
        wx_ref[:, s] = take(k * width, width)
        wh_ref[:, s] = take((3 + k) * width, width)
    w1_ref[...] = take(6 * width, 2 * width)
    w2_ref[...] = take(8 * width, width)
    tail = take(9 * width, 32)
    b1_ref[...] = tail[0:1]
    b2_ref[...] = tail[1:2]
    for k in range(3):
        bias_ref[:, k * width : (k + 1) * width] = tail[16 + k : 17 + k]


def sum_everywhere(pack, scale):
    rows, width = pack.shape
    reps = lax.axis_size("replica")
    group = lax.axis_size("outer") * lax.axis_size("link")
    rep = lax.axis_index("replica")
    chips = reps // 2
    part = rows // reps
    place = jnp.stack([rep // 2, rep % 2]).astype(jnp.int32)
    pairs = [(i, i ^ 1) for i in range(reps)]
    ahead = [[(i, (i + 2 * k) % reps) for i in range(reps)] for k in range(chips)]
    halves = pack.reshape(2, rows // 2, width)
    smem = pl.BlockSpec(memory_space=pltpu.SMEM)
    vmem = pl.BlockSpec(memory_space=pltpu.VMEM)
    other = jnp.where(rep % 2 == 0, halves[1], halves[0])
    got = lax.ppermute(other, "replica", pairs)
    mine = call(
        pair_kernel, (sds((part, width), BF),) * chips, in_specs=[smem, vmem, vmem]
    )(place, pack.reshape(reps, part, width), got.reshape(chips, part, width))
    got = [lax.ppermute(mine[k], "replica", ahead[k]) for k in range(1, chips)]
    mine = sum((g.astype(F32) for g in got), mine[0].astype(F32)).astype(BF)
    mine = total(swap(mine.reshape(group, part // group, width)))
    mine = swap(jnp.broadcast_to(mine[None], (group,) + mine.shape)).reshape(part, width)
    mine = [mine] + [lax.ppermute(mine, "replica", ahead[k]) for k in range(1, chips)]
    got = [lax.ppermute(m, "replica", pairs) for m in mine]
    return call(
        lambda *refs: unpack_kernel(*refs, scale=scale),
        (
            sds((width, 3 * width), F32),
            sds((width, 3 * width), F32),
            sds((1, 3 * width), F32),
            sds((2 * width, width), F32),
            sds((1, width), F32),
            sds((width, width), F32),
            sds((1, width), F32),
        ),
        in_specs=[smem] + [vmem] * (2 * chips),
        scratch_shapes=[pltpu.VMEM((rows, width), BF)],
    )(place, *mine, *got)


def body(
    link_in, path_in, hop_slots, hop_lens, failed, serve_index, link_grad, path_grad,
    gru_wx, gru_wh, gru_bias, mlp_w1, mlp_b1, mlp_w2, mlp_b2,
):
    link_rows = link_in[0]
    links, width = link_rows.shape
    serve_rows = serve_index[0, :, 0, :]
    group, cap = serve_rows.shape
    slots = group * cap
    serve_col = serve_rows.T
    serve_row = serve_rows.reshape(slots // 128, 128)
    flows, hops = hop_slots.shape[1:]
    lens_col = hop_lens[0][:, None]
    slot_col = jnp.where(jnp.arange(hops, dtype=jnp.int32)[None, :] < lens_col, hop_slots[0], -1)
    slot_row = slot_col.T
    keep = (1 - failed[0]).astype(F32)[:, None]
    bias = gru_bias[None]
    wide = 3 * width

    sent = call(serve_kernel, sds((slots, width), BF))(link_rows, serve_col)
    fetched = swap_named(sent, group)
    x, states, part, path_out = call(
        forward_kernel,
        (
            sds((hops, flows, width), BF),
            sds((hops, flows, width), F32),
            sds((slots, width), BF),
            sds((flows, width), BF),
        ),
        scratch_shapes=[
            pltpu.VMEM((hops, flows, wide), F32),
            pltpu.VMEM((hops, flows, width), BF),
        ],
    )(fetched, slot_col, slot_row, lens_col, path_in[0], gru_wx, gru_wh, bias)
    arrived = swap_named(part, group)

    per = 4
    steps = lambda *tail: pl.BlockSpec((per,) + tail, lambda i: (i,) + (0,) * len(tail))
    whole = lambda *shape: pl.BlockSpec(shape, lambda i: (0,) * len(shape))
    coef = call(
        coef_kernel,
        sds((hops, 5, flows, width), F32),
        grid=(hops // per,),
        in_specs=[
            steps(flows, width),
            steps(flows, width),
            whole(flows, 1),
            whole(width, wide),
            whole(width, wide),
            whole(1, wide),
        ],
        out_specs=steps(5, flows, width),
    )(x, states, lens_col, gru_wx, gru_wh, bias)

    sent, agg, act, du, db1 = call(
        link_kernel,
        (
            sds((slots, width), BF),
            sds((links, width), BF),
            sds((links, width), BF),
            sds((links, width), BF),
            sds((1, width), F32),
        ),
    )(arrived, serve_row, serve_col, link_rows, link_grad[0], keep, mlp_w1, mlp_b1[None], mlp_w2)
    returned = swap_named(sent, group)
    link_out, direct, mlp_pack = call(
        link_rest_kernel,
        (
            sds((links, width), BF),
            sds((links, width), F32),
            sds((3 * width + 16, width), BF),
        ),
    )(link_rows, link_grad[0], keep, agg, act, du, db1, mlp_w1, mlp_w2, mlp_b2[None])

    vmem = pl.BlockSpec(memory_space=pltpu.VMEM)
    dpart, path_back, dgi, dgs, db = call(
        backward_kernel,
        (
            sds((slots, width), BF),
            sds((flows, width), F32),
            sds((hops, flows, wide), BF),
            sds((hops, flows, wide), BF),
            sds((8, wide), F32),
        ),
        in_specs=[vmem] * 6 + [pl.BlockSpec(memory_space=pl.ANY)],
        scratch_shapes=[
            pltpu.VMEM((hops, flows, width), BF),
            pltpu.VMEM((hops, 5, flows, width), F32),
            pltpu.VMEM((hops * flows, width), BF),
            pltpu.SemaphoreType.DMA((hops,)),
        ],
    )(returned, slot_col, slot_row, path_grad[0], gru_wx, gru_wh, coef)
    owned = swap_named(dpart, group)

    pack = call(
        weight_kernel,
        sds((10 * width, width), BF),
        grid=(hops // per,),
        in_specs=[
            steps(flows, width),
            steps(flows, width),
            steps(flows, wide),
            steps(flows, wide),
            whole(8, wide),
            whole(3 * width + 16, width),
        ],
        out_specs=whole(10 * width, width),
        scratch_shapes=[pltpu.VMEM((width, wide), F32), pltpu.VMEM((width, wide), F32)],
    )(x, states, dgi, dgs, db, mlp_pack)
    link_back = call(finish_kernel, sds((links, width), F32))(owned, serve_row, direct)

    count = lax.axis_size("replica") * lax.axis_size("outer") * lax.axis_size("link")
    scale = float(count * links) ** (-0.5)
    wx, wh, bias, w1, b1, w2, b2 = sum_everywhere(pack, scale)
    return (
        link_out[None],
        path_out[None],
        link_back[None],
        path_back[None],
        wx,
        wh,
        bias.reshape(wide),
        w1,
        b1.reshape(width),
        w2,
        b2.reshape(width),
    )


def solution(mesh):
    over = P("replica", OL, None)
    flat = P("replica", OL)

    return jax.shard_map(
        body,
        mesh=mesh,
        in_specs=(
            over, over, over, flat, flat, P("replica", None, OL, None), over, over,
            P(), P(), P(), P(), P(), P(), P(),
        ),
        out_specs=(over, over, over, over, P(), P(), P(), P(), P(), P(), P()),
        check_vma=False,
    )
```

```python
import jax
import jax.numpy as jnp
from jax import lax
from jax.experimental import pallas as pl
from jax.experimental.pallas import tpu as pltpu
from jax.sharding import PartitionSpec as P

F32 = jnp.float32
BF = jnp.bfloat16
INTERPRET = False
OL = ("outer", "link")


def dot(a, b):
    return jnp.dot(a, b, preferred_element_type=F32)


def dot_nt(a, b):
    return lax.dot_general(a, b, (((1,), (1,)), ((), ())), preferred_element_type=F32)


def dot_tn(a, b):
    return lax.dot_general(a, b, (((0,), (0,)), ((), ())), preferred_element_type=F32)


def sigmoid(v):
    return 0.5 * jnp.tanh(0.5 * v) + 0.5


def pick_cols(col, width):
    lanes = lax.broadcasted_iota(jnp.int32, (col.shape[0], width), 1)
    return jnp.where(lanes == col, 1.0, 0.0).astype(BF)


def pick_rows(row, height, base=0):
    subs = lax.broadcasted_iota(jnp.int32, (height, row.shape[1]), 0) + base
    return jnp.where(subs == row, 1.0, 0.0).astype(BF)


def call(kernel, outs, mib=16, **kw):
    return pl.pallas_call(
        kernel,
        out_shape=outs,
        interpret=INTERPRET,
        compiler_params=pltpu.CompilerParams(vmem_limit_bytes=mib * 1024 * 1024),
        **kw,
    )


def sds(shape, dtype):
    return jax.ShapeDtypeStruct(shape, dtype)


def send(buf_ref, out_hbm, sem, first, rows, k):
    part = pl.ds(first, rows)
    return pltpu.make_async_copy(buf_ref.at[part, :], out_hbm.at[part, :], sem.at[k])


def gather_rows(table, serve_col, buf_ref, out_hbm, sem, per=8):
    cap, group = serve_col.shape
    links = table.shape[0]
    copies = []
    for k, o in enumerate(range(0, group, per)):
        sel = jnp.concatenate(
            [pick_cols(serve_col[:, i : i + 1], links) for i in range(o, o + per)], axis=0
        )
        buf_ref[o * cap : (o + per) * cap, :] = dot(sel, table).astype(BF)
        copies.append(send(buf_ref, out_hbm, sem, o * cap, per * cap, k))
        copies[-1].start()
    return copies


def serve_kernel(table_ref, col_ref, out_hbm, buf_ref, sem):
    for copy in gather_rows(table_ref[...], jnp.transpose(col_ref[...]), buf_ref, out_hbm, sem):
        copy.wait()


def fetch_hops(table_ref, slot_ref, out_ref, per=4):
    flows, hops = slot_ref.shape
    slots = table_ref.shape[0]
    table = table_ref[...]
    cols = slot_ref[...]
    for t in range(0, hops, per):
        sel = jnp.concatenate(
            [pick_cols(cols[:, k : k + 1], slots) for k in range(t, t + per)], axis=0
        )
        rows = dot(sel, table).astype(out_ref.dtype)
        for k in range(per):
            out_ref[t + k] = rows[k * flows : (k + 1) * flows]


def sum_slots(row_ref, rows, buf_ref, out_hbm, sem, block=512):
    hops = row_ref.shape[0]
    slots = buf_ref.shape[0]
    idx = row_ref[...]
    copies = []
    for k, q in enumerate(range(0, slots, block)):
        sel = jnp.concatenate([pick_rows(idx[t : t + 1, :], block, q) for t in range(hops)], axis=1)
        buf_ref[q : q + block, :] = dot(sel, rows).astype(BF)
        copies.append(send(buf_ref, out_hbm, sem, q, block, k))
        copies[-1].start()
    return copies


def forward_kernel(
    table_ref, slot_ref, row_ref, lens_ref, path_ref, wx_ref, wh_ref, bias_ref,
    x_hbm, state_hbm, prior_hbm, part_hbm, pathout_ref,
    x_ref, state_ref, prior_ref, gi_ref, hb_ref, part_ref, sem, sem_part,
):
    hops, flows, width = x_ref.shape
    outs = [
        pltpu.make_async_copy(x_ref, x_hbm, sem.at[0]),
        pltpu.make_async_copy(state_ref, state_hbm, sem.at[1]),
        pltpu.make_async_copy(prior_ref, prior_hbm, sem.at[2]),
    ]
    fetch_hops(table_ref, slot_ref, x_ref)
    outs[0].start()
    per = 4
    for t in range(0, hops, per):
        rows = x_ref[t : t + per].reshape(per * flows, width)
        gi = dot(rows, wx_ref[...]) + bias_ref[...]
        gi_ref[t : t + per] = gi.reshape(per, flows, 3 * width)
    lens = lens_ref[...]

    def step(t, h):
        state_ref[t] = h
        hb = h.astype(BF)
        prior_ref[t] = hb
        gs = dot(hb, wh_ref[...])
        gi = gi_ref[t]
        z = sigmoid(gi[:, :width] + gs[:, :width])
        r = sigmoid(gi[:, width : 2 * width] + gs[:, width : 2 * width])
        n = jnp.tanh(gi[:, 2 * width :] + r * gs[:, 2 * width :])
        h = jnp.where(t < lens, n + z * (h - n), h)
        hb_ref[t] = h.astype(BF)
        return h

    h = lax.fori_loop(0, hops, step, path_ref[...].astype(F32), unroll=4)
    outs[1].start()
    outs[2].start()
    pathout_ref[...] = h.astype(BF)
    outs += sum_slots(
        row_ref, hb_ref[...].reshape(hops * flows, width), part_ref, part_hbm, sem_part
    )
    for out in outs:
        out.wait()


def coef_kernel(x_ref, state_ref, lens_ref, wx_ref, wh_ref, bias_ref, coef_ref):
    per, flows, width = x_ref.shape
    first = pl.program_id(0) * per
    rows = x_ref[...].reshape(per * flows, width)
    gi = dot(rows, wx_ref[...]) + bias_ref[...]
    h = state_ref[...].reshape(per * flows, width)
    gs = dot(h.astype(BF), wh_ref[...])
    z = sigmoid(gi[:, :width] + gs[:, :width])
    r = sigmoid(gi[:, width : 2 * width] + gs[:, width : 2 * width])
    gs3 = gs[:, 2 * width :]
    n = jnp.tanh(gi[:, 2 * width :] + r * gs3)
    cz = (h - n) * z * (1.0 - z)
    cn = (1.0 - z) * (1.0 - n * n)
    cr = cn * gs3 * r * (1.0 - r)
    for k in range(per):
        live = (first + k) < lens_ref[...]
        s = slice(k * flows, (k + 1) * flows)
        coef_ref[k, 0] = jnp.where(live, z[s], 1.0)
        coef_ref[k, 1] = jnp.where(live, cz[s], 0.0)
        coef_ref[k, 2] = jnp.where(live, cr[s], 0.0)
        coef_ref[k, 3] = jnp.where(live, cn[s], 0.0)
        coef_ref[k, 4] = r[s]


def link_kernel(
    got_ref, srow_ref, scol_ref, link_ref, lgrad_ref, keep_ref, w1_ref, b1_ref, w2_ref,
    out_hbm, mid_hbm, db1_ref,
    buf_ref, mid_ref, sem, sem_out,
):
    links, width = link_ref.shape
    sel = jnp.concatenate(
        [pick_rows(srow_ref[k : k + 1, :], links) for k in range(srow_ref.shape[0])], axis=1
    )
    agg = dot(sel, got_ref[...]).astype(BF)
    mid_ref[:links, :] = agg
    u = dot(link_ref[...], w1_ref[:width, :]) + dot(agg, w1_ref[width:, :]) + b1_ref[...]
    s = sigmoid(u)
    mid_ref[links : 2 * links, :] = (u * s).astype(BF)
    gv = (keep_ref[...] * lgrad_ref[...].astype(F32)).astype(BF)
    du = dot_nt(gv, w2_ref[...]) * s * (1.0 + u * (1.0 - s))
    db1_ref[...] = jnp.sum(du, axis=0, keepdims=True)
    du = du.astype(BF)
    mid_ref[2 * links :, :] = du
    dagg = dot_nt(du, w1_ref[width:, :]).astype(BF)
    copies = [pltpu.make_async_copy(mid_ref, mid_hbm, sem.at[0])]
    copies[0].start()
    copies += gather_rows(dagg, jnp.transpose(scol_ref[...]), buf_ref, out_hbm, sem_out)
    for copy in copies:
        copy.wait()


def link_rest_kernel(
    link_ref, lgrad_ref, keep_ref, mid_ref, db1_ref, w1_ref, w2_ref, b2_ref,
    lout_ref, direct_ref, pack_ref,
):
    links, width = link_ref.shape
    link = link_ref[...]
    keep = keep_ref[...]
    act = mid_ref[links : 2 * links, :]
    du = mid_ref[2 * links :, :]
    value = link.astype(F32) + dot(act, w2_ref[...]) + b2_ref[...]
    lout_ref[...] = (keep * value).astype(BF)
    gv = keep * lgrad_ref[...].astype(F32)
    direct_ref[...] = gv + dot_nt(du, w1_ref[:width, :])
    pack_ref[0:width, :] = dot_tn(link, du).astype(BF)
    pack_ref[width : 2 * width, :] = dot_tn(mid_ref[:links, :], du).astype(BF)
    pack_ref[2 * width : 3 * width, :] = dot_tn(act, gv.astype(BF)).astype(BF)
    db2 = jnp.sum(gv, axis=0, keepdims=True)
    tail = jnp.concatenate([db1_ref[...], db2, jnp.zeros((14, width), F32)], axis=0)
    pack_ref[3 * width :, :] = tail.astype(BF)


def backward_kernel(
    table_ref, slot_ref, row_ref, pgrad_ref, wx_ref, wh_ref, coef_hbm,
    part_hbm, pathgrad_ref, gate_hbm, db_ref,
    hg_ref, coef_ref, gate_ref, dx_ref, part_ref, sem_in, sem_out, sem_part,
):
    hops, flows, width = hg_ref.shape

    def load(t):
        return pltpu.make_async_copy(coef_hbm.at[t], coef_ref.at[t], sem_in.at[t])

    def store(t):
        return pltpu.make_async_copy(gate_ref.at[t], gate_hbm.at[t], sem_out.at[t])

    for t in range(hops - 1, -1, -1):
        load(t).start()
    fetch_hops(table_ref, slot_ref, hg_ref)
    db_ref[...] = jnp.zeros(db_ref.shape, F32)

    def fold(v):
        return jnp.sum(v.reshape(flows // 8, 8, width), axis=0)

    def step(k, g):
        t = hops - 1 - k
        load(t).wait()
        g = g + hg_ref[t].astype(F32)
        az = g * coef_ref[t, 1]
        ar = g * coef_ref[t, 2]
        an = g * coef_ref[t, 3]
        dgs = jnp.concatenate(
            [az.astype(BF), ar.astype(BF), (an * coef_ref[t, 4]).astype(BF)], axis=1
        )
        nxt = g * coef_ref[t, 0] + dot_nt(dgs, wh_ref[...])
        gate_ref[t, :, :width] = an.astype(BF)
        gate_ref[t, :, width:] = dgs
        store(t).start()
        db_ref[:, :width] += fold(az)
        db_ref[:, width : 2 * width] += fold(ar)
        db_ref[:, 2 * width :] += fold(an)
        return nxt

    g = lax.fori_loop(0, hops, step, pgrad_ref[...].astype(F32), unroll=4)
    pathgrad_ref[...] = g
    wx = jnp.concatenate([wx_ref[:, 2 * width :], wx_ref[:, : 2 * width]], axis=1)
    per = 4
    for t in range(0, hops, per):
        rows = gate_ref[t : t + per, :, : 3 * width].reshape(per * flows, 3 * width)
        dx_ref[t * flows : (t + per) * flows, :] = dot_nt(rows, wx).astype(BF)
    for copy in sum_slots(row_ref, dx_ref[...], part_ref, part_hbm, sem_part):
        copy.wait()
    for t in range(hops):
        store(t).wait()


def weight_kernel(
    place_ref, x_ref, prior_ref, gate_ref, db_ref, mlp_ref,
    mine_ref, other_ref, pack_ref, awx_ref, awh_ref,
):
    per, flows, width = x_ref.shape
    i = pl.program_id(0)
    rows = per * flows
    gates = gate_ref[...].reshape(rows, 4 * width)
    gx = dot_tn(x_ref[...].reshape(rows, width), gates[:, : 3 * width])
    gh = dot_tn(prior_ref[...].reshape(rows, width), gates[:, width:])

    @pl.when(i == 0)
    def _():
        awx_ref[...] = gx
        awh_ref[...] = gh

    @pl.when(i > 0)
    def _():
        awx_ref[...] += gx
        awh_ref[...] += gh

    @pl.when(i == pl.num_programs(0) - 1)
    def _():
        for k in range(3):
            s = slice(k * width, (k + 1) * width)
            to = (k + 2) % 3
            pack_ref[to * width : (to + 1) * width, :] = awx_ref[:, s].astype(BF)
            pack_ref[(3 + k) * width : (4 + k) * width, :] = awh_ref[:, s].astype(BF)
        base = 9 * width
        pack_ref[6 * width : base + 16, :] = mlp_ref[...]
        b = jnp.sum(db_ref[...], axis=0, keepdims=True)
        tail = jnp.concatenate(
            [b[:, k * width : (k + 1) * width] for k in range(3)] + [jnp.zeros((13, width), F32)],
            axis=0,
        )
        pack_ref[base + 16 : base + 32, :] = tail.astype(BF)
        rest = pack_ref.shape[0] - base - 32
        pack_ref[base + 32 :, :] = jnp.zeros((rest, width), BF)
        half = mine_ref.shape[0]
        core = place_ref[1]
        mine_ref[...] = pack_ref[pl.ds(pl.multiple_of(core * half, 256), half), :]
        other_ref[...] = pack_ref[pl.ds(pl.multiple_of((1 - core) * half, 256), half), :]


def finish_kernel(got_ref, srow_ref, direct_ref, out_ref):
    links = direct_ref.shape[0]
    sel = jnp.concatenate(
        [pick_rows(srow_ref[k : k + 1, :], links) for k in range(srow_ref.shape[0])], axis=1
    )
    out_ref[...] = direct_ref[...] + dot(sel, got_ref[...])


def swap(blocks, axes=OL, groups=None):
    return lax.all_to_all(
        blocks, axes, split_axis=0, concat_axis=0, tiled=True, axis_index_groups=groups
    )


def swap_named(rows, group):
    return swap(rows.reshape(group, -1, rows.shape[1])).reshape(rows.shape)


def total(v):
    return jnp.sum(v.astype(F32), axis=0).astype(BF)


def pair_kernel(place_ref, pack_ref, got_ref, *out_refs):
    x = place_ref[0]
    chips = len(out_refs)
    part = out_refs[0].shape[0]
    for k in range(chips):
        rows = pl.ds(pl.multiple_of(lax.rem(x + k, chips) * part, 64), part)
        both = pack_ref[rows, :].astype(F32) + got_ref[rows, :].astype(F32)
        out_refs[k][...] = both.astype(BF)


def unpack_kernel(place_ref, *refs, scale):
    x = place_ref[0]
    core = place_ref[1]
    chips = (len(refs) - 8) // 2
    mine = refs[:chips]
    got = refs[chips : 2 * chips]
    wx_ref, wh_ref, bias_ref, w1_ref, b1_ref, w2_ref, b2_ref, all_ref = refs[2 * chips :]
    rows, width = mine[0].shape
    for k in range(chips):
        c = lax.rem(x - k + chips, chips)
        all_ref[pl.ds(pl.multiple_of((core * chips + c) * rows, 64), rows), :] = mine[k][...]
        all_ref[pl.ds(pl.multiple_of(((1 - core) * chips + c) * rows, 64), rows), :] = got[k][...]
    take = lambda a, n: all_ref[a : a + n, :].astype(F32) * scale
    for k in range(3):
        s = slice(k * width, (k + 1) * width)
        wx_ref[:, s] = take(k * width, width)
        wh_ref[:, s] = take((3 + k) * width, width)
    w1_ref[...] = take(6 * width, 2 * width)
    w2_ref[...] = take(8 * width, width)
    tail = take(9 * width, 32)
    b1_ref[...] = tail[0:1]
    b2_ref[...] = tail[1:2]
    for k in range(3):
        bias_ref[k * width : (k + 1) * width] = tail[16 + k]


def whereabouts():
    rep = lax.axis_index("replica")
    return jnp.stack([rep // 2, rep % 2]).astype(jnp.int32)


def sum_everywhere(mine, other, place, scale):
    rows, width = mine.shape
    rows = 2 * rows
    reps = lax.axis_size("replica")
    group = lax.axis_size("outer") * lax.axis_size("link")
    chips = reps // 2
    part = rows // reps
    pairs = [(i, i ^ 1) for i in range(reps)]
    ahead = [[(i, (i + 2 * k) % reps) for i in range(reps)] for k in range(chips)]
    smem = pl.BlockSpec(memory_space=pltpu.SMEM)
    vmem = pl.BlockSpec(memory_space=pltpu.VMEM)
    got = lax.ppermute(other, "replica", pairs)
    mine = call(
        pair_kernel, (sds((part, width), BF),) * chips, in_specs=[smem, vmem, vmem]
    )(place, mine, got)
    got = [lax.ppermute(mine[k], "replica", ahead[k]) for k in range(1, chips)]
    mine = sum((g.astype(F32) for g in got), mine[0].astype(F32)).astype(BF)
    mine = total(swap(mine.reshape(group, part // group, width)))
    mine = swap(jnp.broadcast_to(mine[None], (group,) + mine.shape)).reshape(part, width)
    whole = [mine]
    for k in range(1, chips):
        whole.append(lax.ppermute(mine, "replica", ahead[k]))
    mine = whole
    got = [lax.ppermute(m, "replica", pairs) for m in mine]
    return call(
        lambda *refs: unpack_kernel(*refs, scale=scale),
        (
            sds((width, 3 * width), F32),
            sds((width, 3 * width), F32),
            sds((3 * width,), F32),
            sds((2 * width, width), F32),
            sds((1, width), F32),
            sds((width, width), F32),
            sds((1, width), F32),
        ),
        in_specs=[smem] + [vmem] * (2 * chips),
        scratch_shapes=[pltpu.VMEM((rows, width), BF)],
    )(place, *mine, *got)


def body(
    link_in, path_in, hop_slots, hop_lens, failed, serve_index, link_grad, path_grad,
    gru_wx, gru_wh, gru_bias, mlp_w1, mlp_b1, mlp_w2, mlp_b2,
):
    link_rows = link_in[0]
    links, width = link_rows.shape
    serve_rows = serve_index[0, :, 0, :]
    group, cap = serve_rows.shape
    slots = group * cap
    serve_row = serve_rows.reshape(slots // 128, 128)
    flows, hops = hop_slots.shape[1:]
    lens_col = hop_lens[0][:, None]
    slot_col = jnp.where(jnp.arange(hops, dtype=jnp.int32)[None, :] < lens_col, hop_slots[0], -1)
    slot_row = slot_col.T
    keep = (1 - failed[0]).astype(F32)[:, None]
    bias = gru_bias[None]
    wide = 3 * width

    vmem = pl.BlockSpec(memory_space=pltpu.VMEM)
    smem = pl.BlockSpec(memory_space=pltpu.SMEM)
    hbm = pl.BlockSpec(memory_space=pltpu.HBM)
    blocks = group // 8
    rows_out = [pltpu.VMEM((slots, width), BF)]
    sent = call(
        serve_kernel,
        sds((slots, width), BF),
        out_specs=hbm,
        scratch_shapes=rows_out + [pltpu.SemaphoreType.DMA((blocks,))],
    )(link_rows, serve_rows)
    fetched = swap_named(sent, group)
    place = whereabouts()
    x, states, priors, part, path_out = call(
        forward_kernel,
        (
            sds((hops, flows, width), BF),
            sds((hops, flows, width), F32),
            sds((hops, flows, width), BF),
            sds((slots, width), BF),
            sds((flows, width), BF),
        ),
        mib=62,
        out_specs=[hbm] * 4 + [vmem],
        scratch_shapes=[
            pltpu.VMEM((hops, flows, width), BF),
            pltpu.VMEM((hops, flows, width), F32),
            pltpu.VMEM((hops, flows, width), BF),
            pltpu.VMEM((hops, flows, wide), F32),
            pltpu.VMEM((hops, flows, width), BF),
            *rows_out,
            pltpu.SemaphoreType.DMA((3,)),
            pltpu.SemaphoreType.DMA((slots // 512,)),
        ],
    )(fetched, slot_col, slot_row, lens_col, path_in[0], gru_wx, gru_wh, bias)
    arrived = swap_named(part, group)

    per = 4
    steps = lambda *tail: pl.BlockSpec((per,) + tail, lambda i: (i,) + (0,) * len(tail))
    whole = lambda *shape: pl.BlockSpec(shape, lambda i: (0,) * len(shape))
    coef = call(
        coef_kernel,
        sds((hops, 5, flows, width), F32),
        mib=58,
        grid=(hops // per,),
        in_specs=[
            steps(flows, width),
            steps(flows, width),
            whole(flows, 1),
            whole(width, wide),
            whole(width, wide),
            whole(1, wide),
        ],
        out_specs=steps(5, flows, width),
    )(x, states, lens_col, gru_wx, gru_wh, bias)

    sent, mids, db1 = call(
        link_kernel,
        (
            sds((slots, width), BF),
            sds((3 * links, width), BF),
            sds((1, width), F32),
        ),
        mib=62,
        out_specs=[hbm, hbm, vmem],
        scratch_shapes=rows_out
        + [
            pltpu.VMEM((3 * links, width), BF),
            pltpu.SemaphoreType.DMA((1,)),
            pltpu.SemaphoreType.DMA((blocks,)),
        ],
    )(arrived, serve_row, serve_rows, link_rows, link_grad[0], keep, mlp_w1, mlp_b1[None], mlp_w2)
    returned = swap_named(sent, group)
    link_out, direct, mlp_pack = call(
        link_rest_kernel,
        (
            sds((links, width), BF),
            sds((links, width), F32),
            sds((3 * width + 16, width), BF),
        ),
        mib=58,
    )(link_rows, link_grad[0], keep, mids, db1, mlp_w1, mlp_w2, mlp_b2[None])

    dpart, path_back, gates, db = call(
        backward_kernel,
        (
            sds((slots, width), BF),
            sds((flows, width), F32),
            sds((hops, flows, 4 * width), BF),
            sds((8, wide), F32),
        ),
        mib=51,
        in_specs=[vmem] * 6 + [hbm],
        out_specs=[hbm, vmem, hbm, vmem],
        scratch_shapes=[
            pltpu.VMEM((hops, flows, width), BF),
            pltpu.VMEM((hops, 5, flows, width), F32),
            pltpu.VMEM((hops, flows, 4 * width), BF),
            pltpu.VMEM((hops * flows, width), BF),
            *rows_out,
            pltpu.SemaphoreType.DMA((hops,)),
            pltpu.SemaphoreType.DMA((hops,)),
            pltpu.SemaphoreType.DMA((slots // 512,)),
        ],
    )(returned, slot_col, slot_row, path_grad[0], gru_wx, gru_wh, coef)
    owned = swap_named(dpart, group)

    mine, other = call(
        weight_kernel,
        (sds((5 * width, width), BF),) * 2,
        mib=58,
        grid=(hops // per,),
        in_specs=[
            smem,
            steps(flows, width),
            steps(flows, width),
            steps(flows, 4 * width),
            whole(8, wide),
            whole(3 * width + 16, width),
        ],
        out_specs=[whole(5 * width, width)] * 2,
        scratch_shapes=[
            pltpu.VMEM((10 * width, width), BF),
            pltpu.VMEM((width, wide), F32),
            pltpu.VMEM((width, wide), F32),
        ],
    )(place, x, priors, gates, db, mlp_pack)
    link_back = call(finish_kernel, sds((links, width), F32), mib=58)(owned, serve_row, direct)

    count = lax.axis_size("replica") * lax.axis_size("outer") * lax.axis_size("link")
    scale = float(count * links) ** (-0.5)
    wx, wh, bias, w1, b1, w2, b2 = sum_everywhere(mine, other, place, scale)
    return (
        link_out[None],
        path_out[None],
        link_back[None],
        path_back[None],
        wx,
        wh,
        bias,
        w1,
        b1.reshape(width),
        w2,
        b2.reshape(width),
    )


def solution(mesh):
    over = P("replica", OL, None)
    flat = P("replica", OL)

    return jax.shard_map(
        body,
        mesh=mesh,
        in_specs=(
            over, over, over, flat, flat, P("replica", None, OL, None), over, over,
            P(), P(), P(), P(), P(), P(), P(),
        ),
        out_specs=(over, over, over, over, P(), P(), P(), P(), P(), P(), P()),
        check_vma=False,
    )
```

```python
import jax
import jax.numpy as jnp
from jax import lax
from jax.experimental import pallas as pl
from jax.experimental.pallas import tpu as pltpu
from jax.sharding import PartitionSpec as P

F32 = jnp.float32
BF = jnp.bfloat16
INTERPRET = False
BACK = 49
OL = ("outer", "link")


def dot(a, b):
    return jnp.dot(a, b, preferred_element_type=F32)


def dot_nt(a, b):
    return lax.dot_general(a, b, (((1,), (1,)), ((), ())), preferred_element_type=F32)


def dot_tn(a, b):
    return lax.dot_general(a, b, (((0,), (0,)), ((), ())), preferred_element_type=F32)


def sigmoid(v):
    return 0.5 * jnp.tanh(0.5 * v) + 0.5


def pick_cols(col, width):
    lanes = lax.broadcasted_iota(jnp.int32, (col.shape[0], width), 1)
    return jnp.where(lanes == col, 1.0, 0.0).astype(BF)


def pick_rows(row, height, base=0):
    subs = lax.broadcasted_iota(jnp.int32, (height, row.shape[1]), 0) + base
    return jnp.where(subs == row, 1.0, 0.0).astype(BF)


def call(kernel, outs, mib=16, **kw):
    return pl.pallas_call(
        kernel,
        out_shape=outs,
        interpret=INTERPRET,
        compiler_params=pltpu.CompilerParams(vmem_limit_bytes=mib * 1024 * 1024),
        **kw,
    )


def sds(shape, dtype):
    return jax.ShapeDtypeStruct(shape, dtype)


def send(buf_ref, out_hbm, sem, first, rows, k):
    part = pl.ds(first, rows)
    return pltpu.make_async_copy(buf_ref.at[part, :], out_hbm.at[part, :], sem.at[k])


def gather_rows(table, serve_col, buf_ref, out_hbm, sem, per=8):
    cap, group = serve_col.shape
    links = table.shape[0]
    copies = []
    for k, o in enumerate(range(0, group, per)):
        sel = jnp.concatenate(
            [pick_cols(serve_col[:, i : i + 1], links) for i in range(o, o + per)], axis=0
        )
        buf_ref[o * cap : (o + per) * cap, :] = dot(sel, table).astype(BF)
        copies.append(send(buf_ref, out_hbm, sem, o * cap, per * cap, k))
        copies[-1].start()
    return copies


def serve_kernel(table_ref, col_ref, out_hbm, buf_ref, sem):
    for copy in gather_rows(table_ref[...], jnp.transpose(col_ref[...]), buf_ref, out_hbm, sem):
        copy.wait()


def fetch_hops(table_ref, slot_ref, out_ref, wide_ref, per=4):
    flows, hops = slot_ref.shape
    slots = table_ref.shape[0]
    cols = slot_ref[...]
    for t in range(hops):
        wide_ref[t] = jnp.broadcast_to(cols[:, t : t + 1], (flows, 128))
    lanes = lax.broadcasted_iota(jnp.int32, (per * flows, 128), 1)

    def step(i, carry):
        at = pl.ds(i * per, per)
        idx = wide_ref[at].reshape(per * flows, 128)
        sel = jnp.concatenate(
            [jnp.where(lanes + b == idx, 1.0, 0.0).astype(BF) for b in range(0, slots, 128)],
            axis=1,
        )
        rows = dot(sel, table_ref[...])
        out_ref[at] = rows.reshape(per, flows, rows.shape[1]).astype(out_ref.dtype)
        return carry

    lax.fori_loop(0, hops // per, step, 0, unroll=6)


def sum_slots(row_ref, rows, buf_ref, out_hbm, sem, block=512):
    hops = row_ref.shape[0]
    slots = buf_ref.shape[0]
    idx = row_ref[...]

    def step(k, carry):
        q = pl.multiple_of(k * block, block)
        sel = jnp.concatenate([pick_rows(idx[t : t + 1, :], block, q) for t in range(hops)], axis=1)
        buf_ref[pl.ds(q, block), :] = dot(sel, rows).astype(BF)
        send(buf_ref, out_hbm, sem, q, block, k).start()
        return carry

    lax.fori_loop(0, slots // block, step, 0, unroll=1)
    return [send(buf_ref, out_hbm, sem, k * block, block, k) for k in range(slots // block)]


def forward_kernel(
    table_ref, slot_ref, row_ref, lens_ref, path_ref, wx_ref, wh_ref, bias_ref,
    x_hbm, state_hbm, prior_hbm, part_hbm, pathout_ref,
    x_ref, state_ref, prior_ref, gi_ref, hb_ref, part_ref, wide_ref, sem, sem_part,
):
    hops, flows, width = x_ref.shape
    outs = [
        pltpu.make_async_copy(x_ref, x_hbm, sem.at[0]),
        pltpu.make_async_copy(state_ref, state_hbm, sem.at[1]),
        pltpu.make_async_copy(prior_ref, prior_hbm, sem.at[2]),
    ]
    fetch_hops(table_ref, slot_ref, x_ref, wide_ref)
    outs[0].start()
    per = 4
    for t in range(0, hops, per):
        rows = x_ref[t : t + per].reshape(per * flows, width)
        gi = dot(rows, wx_ref[...]) + bias_ref[...]
        gi_ref[t : t + per] = gi.reshape(per, flows, 3 * width)
    lens = lens_ref[...]

    def step(t, h):
        state_ref[t] = h
        hb = h.astype(BF)
        prior_ref[t] = hb
        gs = dot(hb, wh_ref[...])
        gi = gi_ref[t]
        z = sigmoid(gi[:, :width] + gs[:, :width])
        r = sigmoid(gi[:, width : 2 * width] + gs[:, width : 2 * width])
        n = jnp.tanh(gi[:, 2 * width :] + r * gs[:, 2 * width :])
        h = jnp.where(t < lens, n + z * (h - n), h)
        hb_ref[t] = h.astype(BF)
        return h

    h = lax.fori_loop(0, hops, step, path_ref[...].astype(F32), unroll=2)
    outs[1].start()
    outs[2].start()
    pathout_ref[...] = h.astype(BF)
    outs += sum_slots(
        row_ref, hb_ref[...].reshape(hops * flows, width), part_ref, part_hbm, sem_part
    )
    for out in outs:
        out.wait()


def coef_kernel(x_ref, state_ref, lens_ref, wx_ref, wh_ref, bias_ref, coef_ref):
    per, flows, width = x_ref.shape
    first = pl.program_id(0) * per
    rows = x_ref[...].reshape(per * flows, width)
    gi = dot(rows, wx_ref[...]) + bias_ref[...]
    h = state_ref[...].reshape(per * flows, width)
    gs = dot(h.astype(BF), wh_ref[...])
    z = sigmoid(gi[:, :width] + gs[:, :width])
    r = sigmoid(gi[:, width : 2 * width] + gs[:, width : 2 * width])
    gs3 = gs[:, 2 * width :]
    n = jnp.tanh(gi[:, 2 * width :] + r * gs3)
    cz = (h - n) * z * (1.0 - z)
    cn = (1.0 - z) * (1.0 - n * n)
    cr = cn * gs3 * r * (1.0 - r)
    for k in range(per):
        live = (first + k) < lens_ref[...]
        s = slice(k * flows, (k + 1) * flows)
        coef_ref[k, 0] = jnp.where(live, z[s], 1.0)
        coef_ref[k, 1] = jnp.where(live, cz[s], 0.0)
        coef_ref[k, 2] = jnp.where(live, cr[s], 0.0)
        coef_ref[k, 3] = jnp.where(live, cn[s], 0.0)
        coef_ref[k, 4] = r[s]


def link_kernel(
    got_ref, srow_ref, scol_ref, link_ref, lgrad_ref, keep_ref, w1_ref, b1_ref, w2_ref,
    out_hbm, mid_hbm, db1_ref,
    buf_ref, mid_ref, sem, sem_out,
):
    links, width = link_ref.shape
    sel = jnp.concatenate(
        [pick_rows(srow_ref[k : k + 1, :], links) for k in range(srow_ref.shape[0])], axis=1
    )
    agg = dot(sel, got_ref[...]).astype(BF)
    mid_ref[:links, :] = agg
    u = dot(link_ref[...], w1_ref[:width, :]) + dot(agg, w1_ref[width:, :]) + b1_ref[...]
    s = sigmoid(u)
    mid_ref[links : 2 * links, :] = (u * s).astype(BF)
    gv = (keep_ref[...] * lgrad_ref[...].astype(F32)).astype(BF)
    du = dot_nt(gv, w2_ref[...]) * s * (1.0 + u * (1.0 - s))
    db1_ref[...] = jnp.sum(du, axis=0, keepdims=True)
    du = du.astype(BF)
    mid_ref[2 * links :, :] = du
    dagg = dot_nt(du, w1_ref[width:, :]).astype(BF)
    copies = [pltpu.make_async_copy(mid_ref, mid_hbm, sem.at[0])]
    copies[0].start()
    copies += gather_rows(dagg, jnp.transpose(scol_ref[...]), buf_ref, out_hbm, sem_out)
    for copy in copies:
        copy.wait()


def link_rest_kernel(
    link_ref, lgrad_ref, keep_ref, mid_ref, db1_ref, w1_ref, w2_ref, b2_ref,
    lout_ref, direct_ref, pack_ref,
):
    links, width = link_ref.shape
    link = link_ref[...]
    keep = keep_ref[...]
    act = mid_ref[links : 2 * links, :]
    du = mid_ref[2 * links :, :]
    value = link.astype(F32) + dot(act, w2_ref[...]) + b2_ref[...]
    lout_ref[...] = (keep * value).astype(BF)
    gv = keep * lgrad_ref[...].astype(F32)
    direct_ref[...] = gv + dot_nt(du, w1_ref[:width, :])
    pack_ref[0:width, :] = dot_tn(link, du).astype(BF)
    pack_ref[width : 2 * width, :] = dot_tn(mid_ref[:links, :], du).astype(BF)
    pack_ref[2 * width : 3 * width, :] = dot_tn(act, gv.astype(BF)).astype(BF)
    db2 = jnp.sum(gv, axis=0, keepdims=True)
    tail = jnp.concatenate([db1_ref[...], db2, jnp.zeros((14, width), F32)], axis=0)
    pack_ref[3 * width :, :] = tail.astype(BF)


def backward_kernel(
    place_ref, table_ref, slot_ref, pgrad_ref, wx_ref, wh_ref, mlp_hbm, coef_hbm, x_hbm, prior_hbm,
    pathgrad_ref, dx_hbm, mine_ref, other_ref,
    hg_ref, coef_ref, gate_ref, dx_ref, x_ref, prior_ref, pack_ref, db_ref, wide_ref, sem_in, sem,
):
    hops, flows, width = hg_ref.shape
    rows = hops * flows

    def load(t):
        return pltpu.make_async_copy(coef_hbm.at[t], coef_ref.at[t], sem_in.at[t])

    for t in range(hops - 1, -1, -1):
        load(t).start()
    extra = [
        pltpu.make_async_copy(x_hbm, x_ref, sem.at[0]),
        pltpu.make_async_copy(prior_hbm, prior_ref, sem.at[1]),
        pltpu.make_async_copy(
            mlp_hbm, pack_ref.at[pl.ds(6 * width, mlp_hbm.shape[0]), :], sem.at[3]
        ),
    ]
    for copy in extra:
        copy.start()
    fetch_hops(table_ref, slot_ref, hg_ref, wide_ref)
    db_ref[...] = jnp.zeros(db_ref.shape, F32)

    def fold(v):
        return jnp.sum(v.reshape(flows // 8, 8, width), axis=0)

    def step(k, g):
        t = hops - 1 - k
        load(t).wait()
        g = g + hg_ref[t].astype(F32)
        az = g * coef_ref[t, 1]
        ar = g * coef_ref[t, 2]
        an = g * coef_ref[t, 3]
        anb = an.astype(BF)
        azb = az.astype(BF)
        arb = ar.astype(BF)
        cnb = (an * coef_ref[t, 4]).astype(BF)
        nxt = g * coef_ref[t, 0] + dot_nt(jnp.concatenate([azb, arb, cnb], axis=1), wh_ref[...])
        for k, gate in enumerate((anb, azb, arb, cnb)):
            gate_ref[k, t] = gate
        dx_ref[t] = dot_nt(jnp.concatenate([azb, arb, anb], axis=1), wx_ref[...]).astype(BF)
        db_ref[:, :width] += fold(az)
        db_ref[:, width : 2 * width] += fold(ar)
        db_ref[:, 2 * width :] += fold(an)
        return nxt

    g = lax.fori_loop(0, hops, step, pgrad_ref[...].astype(F32), unroll=2)
    dx_out = pltpu.make_async_copy(dx_ref, dx_hbm, sem.at[2])
    dx_out.start()
    pathgrad_ref[...] = g
    for copy in extra:
        copy.wait()
    base = 9 * width

    def outer(k, carry):
        to = pl.multiple_of(lax.rem(k + 2, 3) * width, width)
        col = gate_ref[k].reshape(rows, width)
        pack_ref[pl.ds(to, width), :] = dot_tn(x_ref[...].reshape(rows, width), col).astype(BF)
        to = pl.multiple_of((k + 3) * width, width)
        col = gate_ref[k + 1].reshape(rows, width)
        pack_ref[pl.ds(to, width), :] = dot_tn(prior_ref[...].reshape(rows, width), col).astype(BF)
        return carry

    lax.fori_loop(0, 3, outer, 0, unroll=1)
    b = jnp.sum(db_ref[...], axis=0, keepdims=True)
    tail = jnp.concatenate(
        [b[:, k * width : (k + 1) * width] for k in range(3)] + [jnp.zeros((13, width), F32)],
        axis=0,
    )
    pack_ref[base + 16 : base + 32, :] = tail.astype(BF)
    pack_ref[base + 32 :, :] = jnp.zeros((pack_ref.shape[0] - base - 32, width), BF)
    half = mine_ref.shape[0]
    core = place_ref[1]
    mine_ref[...] = pack_ref[pl.ds(pl.multiple_of(core * half, 256), half), :]
    other_ref[...] = pack_ref[pl.ds(pl.multiple_of((1 - core) * half, 256), half), :]
    dx_out.wait()


def sums_kernel(row_ref, dx_ref, out_hbm, buf_ref, sem):
    hops, flows, width = dx_ref.shape
    rows = dx_ref[...].reshape(hops * flows, width)
    for copy in sum_slots(row_ref, rows, buf_ref, out_hbm, sem):
        copy.wait()


def finish_kernel(got_ref, srow_ref, direct_ref, out_ref):
    links = direct_ref.shape[0]
    sel = jnp.concatenate(
        [pick_rows(srow_ref[k : k + 1, :], links) for k in range(srow_ref.shape[0])], axis=1
    )
    out_ref[...] = direct_ref[...] + dot(sel, got_ref[...])


def swap(blocks, axes=OL, groups=None):
    return lax.all_to_all(
        blocks, axes, split_axis=0, concat_axis=0, tiled=True, axis_index_groups=groups
    )


def swap_named(rows, group):
    return swap(rows.reshape(group, -1, rows.shape[1])).reshape(rows.shape)


def total(v):
    return jnp.sum(v.astype(F32), axis=0).astype(BF)


def pair_kernel(place_ref, pack_ref, got_ref, *out_refs):
    x = place_ref[0]
    chips = len(out_refs)
    part = out_refs[0].shape[0]
    for k in range(chips):
        rows = pl.ds(pl.multiple_of(lax.rem(x + k, chips) * part, 64), part)
        both = pack_ref[rows, :].astype(F32) + got_ref[rows, :].astype(F32)
        out_refs[k][...] = both.astype(BF)


def link_join_kernel(place_ref, *refs):
    out_ref = refs[-1]
    count = out_ref.shape[0]
    for k in range(count):
        out_ref[lax.rem(place_ref[3] - k + count, count)] = refs[k][...]


def outer_join_kernel(place_ref, *refs):
    out_ref = refs[-1]
    count = len(refs) - 1
    rows = refs[0].shape[0]
    for k in range(count):
        to = lax.rem(place_ref[2] - k + count, count)
        out_ref[pl.ds(pl.multiple_of(to * rows, 16), rows), :] = refs[k][...]


def around(piece, axis):
    count = lax.axis_size(axis)
    got = [piece]
    for k in range(1, count):
        got.append(lax.ppermute(piece, axis, [(i, (i + k) % count) for i in range(count)]))
    return got


def unpack_kernel(place_ref, *refs, scale):
    x = place_ref[0]
    core = place_ref[1]
    chips = (len(refs) - 8) // 2
    mine = refs[:chips]
    got = refs[chips : 2 * chips]
    wx_ref, wh_ref, bias_ref, w1_ref, b1_ref, w2_ref, b2_ref, all_ref = refs[2 * chips :]
    rows, width = mine[0].shape
    for k in range(chips):
        c = lax.rem(x - k + chips, chips)
        all_ref[pl.ds(pl.multiple_of((core * chips + c) * rows, 64), rows), :] = mine[k][...]
        all_ref[pl.ds(pl.multiple_of(((1 - core) * chips + c) * rows, 64), rows), :] = got[k][...]
    take = lambda a, n: all_ref[a : a + n, :].astype(F32) * scale
    for k in range(3):
        s = slice(k * width, (k + 1) * width)
        wx_ref[:, s] = take(k * width, width)
        wh_ref[:, s] = take((3 + k) * width, width)
    w1_ref[...] = take(6 * width, 2 * width)
    w2_ref[...] = take(8 * width, width)
    tail = take(9 * width, 32)
    b1_ref[...] = tail[0:1]
    b2_ref[...] = tail[1:2]
    for k in range(3):
        bias_ref[k * width : (k + 1) * width] = tail[16 + k]


def whereabouts():
    rep = lax.axis_index("replica")
    spots = [rep // 2, rep % 2, lax.axis_index("outer"), lax.axis_index("link")]
    return jnp.stack(spots).astype(jnp.int32)


def sum_everywhere(mine, other, place, scale):
    rows, width = mine.shape
    rows = 2 * rows
    reps = lax.axis_size("replica")
    group = lax.axis_size("outer") * lax.axis_size("link")
    chips = reps // 2
    part = rows // reps
    pairs = [(i, i ^ 1) for i in range(reps)]
    ahead = [[(i, (i + 2 * k) % reps) for i in range(reps)] for k in range(chips)]
    smem = pl.BlockSpec(memory_space=pltpu.SMEM)
    vmem = pl.BlockSpec(memory_space=pltpu.VMEM)
    got = lax.ppermute(other, "replica", pairs)
    mine = call(
        pair_kernel, (sds((part, width), BF),) * chips, in_specs=[smem, vmem, vmem]
    )(place, mine, got)
    got = []
    for k in range(1, chips):
        got.append(lax.ppermute(mine[k], "replica", ahead[k]))
    mine = sum((g.astype(F32) for g in got), mine[0].astype(F32)).astype(BF)
    mine = total(swap(mine.reshape(group, part // group, width)))
    got = around(mine, "link")
    mine = call(
        link_join_kernel, sds((len(got),) + mine.shape, BF), in_specs=[smem] + [vmem] * len(got)
    )(place, *got).reshape(-1, width)
    got = around(mine, "outer")
    mine = call(
        outer_join_kernel, sds((part, width), BF), in_specs=[smem] + [vmem] * len(got)
    )(place, *got)
    whole = [mine]
    for k in range(1, chips):
        whole.append(lax.ppermute(mine, "replica", ahead[k]))
    mine = whole
    got = [lax.ppermute(m, "replica", pairs) for m in mine]
    return call(
        lambda *refs: unpack_kernel(*refs, scale=scale),
        (
            sds((width, 3 * width), F32),
            sds((width, 3 * width), F32),
            sds((3 * width,), F32),
            sds((2 * width, width), F32),
            sds((1, width), F32),
            sds((width, width), F32),
            sds((1, width), F32),
        ),
        in_specs=[smem] + [vmem] * (2 * chips),
        scratch_shapes=[pltpu.VMEM((rows, width), BF)],
    )(place, *mine, *got)


def body(
    link_in, path_in, hop_slots, hop_lens, failed, serve_index, link_grad, path_grad,
    gru_wx, gru_wh, gru_bias, mlp_w1, mlp_b1, mlp_w2, mlp_b2,
):
    link_rows = link_in[0]
    links, width = link_rows.shape
    serve_rows = serve_index[0, :, 0, :]
    group, cap = serve_rows.shape
    slots = group * cap
    serve_row = serve_rows.reshape(slots // 128, 128)
    flows, hops = hop_slots.shape[1:]
    lens_col = hop_lens[0][:, None]
    slot_col = jnp.where(jnp.arange(hops, dtype=jnp.int32)[None, :] < lens_col, hop_slots[0], -1)
    slot_row = slot_col.T
    keep = (1 - failed[0]).astype(F32)[:, None]
    bias = gru_bias[None]
    wide = 3 * width

    vmem = pl.BlockSpec(memory_space=pltpu.VMEM)
    smem = pl.BlockSpec(memory_space=pltpu.SMEM)
    hbm = pl.BlockSpec(memory_space=pltpu.HBM)
    blocks = group // 8
    rows_out = [pltpu.VMEM((slots, width), BF)]
    sent = call(
        serve_kernel,
        sds((slots, width), BF),
        out_specs=hbm,
        scratch_shapes=rows_out + [pltpu.SemaphoreType.DMA((blocks,))],
    )(link_rows, serve_rows)
    fetched = swap_named(sent, group)
    place = whereabouts()
    x, states, priors, part, path_out = call(
        forward_kernel,
        (
            sds((hops, flows, width), BF),
            sds((hops, flows, width), F32),
            sds((hops, flows, width), BF),
            sds((slots, width), BF),
            sds((flows, width), BF),
        ),
        mib=62,
        out_specs=[hbm] * 4 + [vmem],
        scratch_shapes=[
            pltpu.VMEM((hops, flows, width), BF),
            pltpu.VMEM((hops, flows, width), F32),
            pltpu.VMEM((hops, flows, width), BF),
            pltpu.VMEM((hops, flows, wide), F32),
            pltpu.VMEM((hops, flows, width), BF),
            *rows_out,
            pltpu.VMEM((hops, flows, 128), jnp.int32),
            pltpu.SemaphoreType.DMA((3,)),
            pltpu.SemaphoreType.DMA((slots // 512,)),
        ],
    )(fetched, slot_col, slot_row, lens_col, path_in[0], gru_wx, gru_wh, bias)
    arrived = swap_named(part, group)

    per = 2
    steps = lambda *tail: pl.BlockSpec((per,) + tail, lambda i: (i,) + (0,) * len(tail))
    whole = lambda *shape: pl.BlockSpec(shape, lambda i: (0,) * len(shape))
    coef = call(
        coef_kernel,
        sds((hops, 5, flows, width), F32),
        mib=58,
        grid=(hops // per,),
        in_specs=[
            steps(flows, width),
            steps(flows, width),
            whole(flows, 1),
            whole(width, wide),
            whole(width, wide),
            whole(1, wide),
        ],
        out_specs=steps(5, flows, width),
    )(x, states, lens_col, gru_wx, gru_wh, bias)

    sent, mids, db1 = call(
        link_kernel,
        (
            sds((slots, width), BF),
            sds((3 * links, width), BF),
            sds((1, width), F32),
        ),
        mib=62,
        out_specs=[hbm, hbm, vmem],
        scratch_shapes=rows_out
        + [
            pltpu.VMEM((3 * links, width), BF),
            pltpu.SemaphoreType.DMA((1,)),
            pltpu.SemaphoreType.DMA((blocks,)),
        ],
    )(arrived, serve_row, serve_rows, link_rows, link_grad[0], keep, mlp_w1, mlp_b1[None], mlp_w2)
    returned = swap_named(sent, group)
    link_out, direct, mlp_pack = call(
        link_rest_kernel,
        (
            sds((links, width), BF),
            sds((links, width), F32),
            sds((3 * width + 16, width), BF),
        ),
        mib=58,
    )(link_rows, link_grad[0], keep, mids, db1, mlp_w1, mlp_w2, mlp_b2[None])

    path_back, dx, mine, other = call(
        backward_kernel,
        (
            sds((flows, width), F32),
            sds((hops, flows, width), BF),
            sds((5 * width, width), BF),
            sds((5 * width, width), BF),
        ),
        mib=BACK,
        in_specs=[smem] + [vmem] * 5 + [hbm] * 4,
        out_specs=[vmem, hbm, vmem, vmem],
        scratch_shapes=[
            pltpu.VMEM((hops, flows, width), BF),
            pltpu.VMEM((hops, 5, flows, width), F32),
            pltpu.VMEM((4, hops, flows, width), BF),
            pltpu.VMEM((hops, flows, width), BF),
            pltpu.VMEM((hops, flows, width), BF),
            pltpu.VMEM((hops, flows, width), BF),
            pltpu.VMEM((10 * width, width), BF),
            pltpu.VMEM((8, wide), F32),
            pltpu.VMEM((hops, flows, 128), jnp.int32),
            pltpu.SemaphoreType.DMA((hops,)),
            pltpu.SemaphoreType.DMA((4,)),
        ],
    )(place, returned, slot_col, path_grad[0], gru_wx, gru_wh, mlp_pack, coef, x, priors)
    dpart = call(
        sums_kernel,
        sds((slots, width), BF),
        mib=58,
        out_specs=hbm,
        scratch_shapes=rows_out + [pltpu.SemaphoreType.DMA((slots // 512,))],
    )(slot_row, dx)
    owned = swap_named(dpart, group)
    link_back = call(finish_kernel, sds((links, width), F32), mib=58)(owned, serve_row, direct)

    count = lax.axis_size("replica") * lax.axis_size("outer") * lax.axis_size("link")
    scale = float(count * links) ** (-0.5)
    wx, wh, bias, w1, b1, w2, b2 = sum_everywhere(mine, other, place, scale)
    return (
        link_out[None],
        path_out[None],
        link_back[None],
        path_back[None],
        wx,
        wh,
        bias,
        w1,
        b1.reshape(width),
        w2,
        b2.reshape(width),
    )


def solution(mesh):
    over = P("replica", OL, None)
    flat = P("replica", OL)

    return jax.shard_map(
        body,
        mesh=mesh,
        in_specs=(
            over, over, over, flat, flat, P("replica", None, OL, None), over, over,
            P(), P(), P(), P(), P(), P(), P(),
        ),
        out_specs=(over, over, over, over, P(), P(), P(), P(), P(), P(), P()),
        check_vma=False,
    )
```

```python
import jax
import jax.numpy as jnp
from jax import lax
from jax.experimental import pallas as pl
from jax.experimental.pallas import tpu as pltpu
from jax.sharding import PartitionSpec as P

F32 = jnp.float32
BF = jnp.bfloat16
INTERPRET = False
OL = ("outer", "link")


def dot(a, b):
    return jnp.dot(a, b, preferred_element_type=F32)


def dot_nt(a, b):
    return lax.dot_general(a, b, (((1,), (1,)), ((), ())), preferred_element_type=F32)


def dot_tn(a, b):
    return lax.dot_general(a, b, (((0,), (0,)), ((), ())), preferred_element_type=F32)


def sigmoid(v):
    return 0.5 * jnp.tanh(0.5 * v) + 0.5


def pick_cols(col, width):
    lanes = lax.broadcasted_iota(jnp.int32, (col.shape[0], width), 1)
    return jnp.where(lanes == col, 1.0, 0.0).astype(BF)


def pick_rows(row, height, base=0):
    subs = lax.broadcasted_iota(jnp.int32, (height, row.shape[1]), 0) + base
    return jnp.where(subs == row, 1.0, 0.0).astype(BF)


def call(kernel, outs, mib=16, **kw):
    return pl.pallas_call(
        kernel,
        out_shape=outs,
        interpret=INTERPRET,
        compiler_params=pltpu.CompilerParams(vmem_limit_bytes=mib * 1024 * 1024),
        **kw,
    )


def sds(shape, dtype):
    return jax.ShapeDtypeStruct(shape, dtype)


def send(buf_ref, out_hbm, sem, first, rows, k):
    part = pl.ds(first, rows)
    return pltpu.make_async_copy(buf_ref.at[part, :], out_hbm.at[part, :], sem.at[k])


def gather_rows(table, serve_col, buf_ref, out_hbm, sem, per=8):
    cap, group = serve_col.shape
    links = table.shape[0]
    copies = []
    for k, o in enumerate(range(0, group, per)):
        sel = jnp.concatenate(
            [pick_cols(serve_col[:, i : i + 1], links) for i in range(o, o + per)], axis=0
        )
        buf_ref[o * cap : (o + per) * cap, :] = dot(sel, table).astype(BF)
        copies.append(send(buf_ref, out_hbm, sem, o * cap, per * cap, k))
        copies[-1].start()
    return copies


def serve_kernel(table_ref, col_ref, out_hbm, buf_ref, sem):
    for copy in gather_rows(table_ref[...], jnp.transpose(col_ref[...]), buf_ref, out_hbm, sem):
        copy.wait()


def fetch_hops(table_ref, slot_ref, out_ref, per=4):
    flows, hops = slot_ref.shape
    slots = table_ref.shape[0]
    table = table_ref[...]
    cols = slot_ref[...]
    for t in range(0, hops, per):
        sel = jnp.concatenate(
            [pick_cols(cols[:, k : k + 1], slots) for k in range(t, t + per)], axis=0
        )
        rows = dot(sel, table).astype(out_ref.dtype)
        for k in range(per):
            out_ref[t + k] = rows[k * flows : (k + 1) * flows]


def sum_slots(row_ref, rows, buf_ref, out_hbm, sem, block=512):
    hops = row_ref.shape[0]
    slots = buf_ref.shape[0]
    idx = row_ref[...]

    def step(k, carry):
        q = pl.multiple_of(k * block, block)
        sel = jnp.concatenate([pick_rows(idx[t : t + 1, :], block, q) for t in range(hops)], axis=1)
        buf_ref[pl.ds(q, block), :] = dot(sel, rows).astype(BF)
        send(buf_ref, out_hbm, sem, q, block, k).start()
        return carry

    lax.fori_loop(0, slots // block, step, 0, unroll=2)
    return [send(buf_ref, out_hbm, sem, k * block, block, k) for k in range(slots // block)]


def forward_kernel(
    table_ref, slot_ref, row_ref, lens_ref, path_ref, wx_ref, wh_ref, bias_ref,
    x_hbm, state_hbm, prior_hbm, part_hbm, pathout_ref,
    x_ref, state_ref, prior_ref, gi_ref, hb_ref, part_ref, sem, sem_part,
):
    hops, flows, width = x_ref.shape
    outs = [
        pltpu.make_async_copy(x_ref, x_hbm, sem.at[0]),
        pltpu.make_async_copy(state_ref, state_hbm, sem.at[1]),
        pltpu.make_async_copy(prior_ref, prior_hbm, sem.at[2]),
    ]
    fetch_hops(table_ref, slot_ref, x_ref)
    outs[0].start()
    per = 4
    for t in range(0, hops, per):
        rows = x_ref[t : t + per].reshape(per * flows, width)
        gi = dot(rows, wx_ref[...]) + bias_ref[...]
        gi_ref[t : t + per] = gi.reshape(per, flows, 3 * width)
    lens = lens_ref[...]

    def step(t, h):
        state_ref[t] = h
        hb = h.astype(BF)
        prior_ref[t] = hb
        gs = dot(hb, wh_ref[...])
        gi = gi_ref[t]
        z = sigmoid(gi[:, :width] + gs[:, :width])
        r = sigmoid(gi[:, width : 2 * width] + gs[:, width : 2 * width])
        n = jnp.tanh(gi[:, 2 * width :] + r * gs[:, 2 * width :])
        h = jnp.where(t < lens, n + z * (h - n), h)
        hb_ref[t] = h.astype(BF)
        return h

    h = lax.fori_loop(0, hops, step, path_ref[...].astype(F32), unroll=4)
    outs[1].start()
    outs[2].start()
    pathout_ref[...] = h.astype(BF)
    outs += sum_slots(
        row_ref, hb_ref[...].reshape(hops * flows, width), part_ref, part_hbm, sem_part
    )
    for out in outs:
        out.wait()


def coef_kernel(x_ref, state_ref, lens_ref, wx_ref, wh_ref, bias_ref, coef_ref):
    per, flows, width = x_ref.shape
    first = pl.program_id(0) * per
    rows = x_ref[...].reshape(per * flows, width)
    gi = dot(rows, wx_ref[...]) + bias_ref[...]
    h = state_ref[...].reshape(per * flows, width)
    gs = dot(h.astype(BF), wh_ref[...])
    z = sigmoid(gi[:, :width] + gs[:, :width])
    r = sigmoid(gi[:, width : 2 * width] + gs[:, width : 2 * width])
    gs3 = gs[:, 2 * width :]
    n = jnp.tanh(gi[:, 2 * width :] + r * gs3)
    cz = (h - n) * z * (1.0 - z)
    cn = (1.0 - z) * (1.0 - n * n)
    cr = cn * gs3 * r * (1.0 - r)
    for k in range(per):
        live = (first + k) < lens_ref[...]
        s = slice(k * flows, (k + 1) * flows)
        coef_ref[k, 0] = jnp.where(live, z[s], 1.0)
        coef_ref[k, 1] = jnp.where(live, cz[s], 0.0)
        coef_ref[k, 2] = jnp.where(live, cr[s], 0.0)
        coef_ref[k, 3] = jnp.where(live, cn[s], 0.0)
        coef_ref[k, 4] = r[s]


def link_kernel(
    got_ref, srow_ref, scol_ref, link_ref, lgrad_ref, keep_ref, w1_ref, b1_ref, w2_ref,
    out_hbm, mid_hbm, db1_ref,
    buf_ref, mid_ref, sem, sem_out,
):
    links, width = link_ref.shape
    sel = jnp.concatenate(
        [pick_rows(srow_ref[k : k + 1, :], links) for k in range(srow_ref.shape[0])], axis=1
    )
    agg = dot(sel, got_ref[...]).astype(BF)
    mid_ref[:links, :] = agg
    u = dot(link_ref[...], w1_ref[:width, :]) + dot(agg, w1_ref[width:, :]) + b1_ref[...]
    s = sigmoid(u)
    mid_ref[links : 2 * links, :] = (u * s).astype(BF)
    gv = (keep_ref[...] * lgrad_ref[...].astype(F32)).astype(BF)
    du = dot_nt(gv, w2_ref[...]) * s * (1.0 + u * (1.0 - s))
    db1_ref[...] = jnp.sum(du, axis=0, keepdims=True)
    du = du.astype(BF)
    mid_ref[2 * links :, :] = du
    dagg = dot_nt(du, w1_ref[width:, :]).astype(BF)
    copies = [pltpu.make_async_copy(mid_ref, mid_hbm, sem.at[0])]
    copies[0].start()
    copies += gather_rows(dagg, jnp.transpose(scol_ref[...]), buf_ref, out_hbm, sem_out)
    for copy in copies:
        copy.wait()


def link_rest_kernel(
    link_ref, lgrad_ref, keep_ref, mid_ref, db1_ref, w1_ref, w2_ref, b2_ref,
    lout_ref, direct_ref, pack_ref,
):
    links, width = link_ref.shape
    link = link_ref[...]
    keep = keep_ref[...]
    act = mid_ref[links : 2 * links, :]
    du = mid_ref[2 * links :, :]
    value = link.astype(F32) + dot(act, w2_ref[...]) + b2_ref[...]
    lout_ref[...] = (keep * value).astype(BF)
    gv = keep * lgrad_ref[...].astype(F32)
    direct_ref[...] = gv + dot_nt(du, w1_ref[:width, :])
    pack_ref[0:width, :] = dot_tn(link, du).astype(BF)
    pack_ref[width : 2 * width, :] = dot_tn(mid_ref[:links, :], du).astype(BF)
    pack_ref[2 * width : 3 * width, :] = dot_tn(act, gv.astype(BF)).astype(BF)
    db2 = jnp.sum(gv, axis=0, keepdims=True)
    tail = jnp.concatenate([db1_ref[...], db2, jnp.zeros((14, width), F32)], axis=0)
    pack_ref[3 * width :, :] = tail.astype(BF)


def backward_kernel(
    table_ref, slot_ref, row_ref, pgrad_ref, wx_ref, wh_ref, coef_hbm,
    part_hbm, pathgrad_ref, gate_hbm, db_ref,
    hg_ref, coef_ref, gate_ref, dx_ref, part_ref, sem_in, sem_out, sem_part,
):
    hops, flows, width = hg_ref.shape

    def load(t):
        return pltpu.make_async_copy(coef_hbm.at[t], coef_ref.at[t], sem_in.at[t])

    def store(t):
        return pltpu.make_async_copy(gate_ref.at[t], gate_hbm.at[t], sem_out.at[t])

    for t in range(hops - 1, -1, -1):
        load(t).start()
    fetch_hops(table_ref, slot_ref, hg_ref)
    db_ref[...] = jnp.zeros(db_ref.shape, F32)

    def fold(v):
        return jnp.sum(v.reshape(flows // 8, 8, width), axis=0)

    def step(k, g):
        t = hops - 1 - k
        load(t).wait()
        g = g + hg_ref[t].astype(F32)
        az = g * coef_ref[t, 1]
        ar = g * coef_ref[t, 2]
        an = g * coef_ref[t, 3]
        dgs = jnp.concatenate(
            [az.astype(BF), ar.astype(BF), (an * coef_ref[t, 4]).astype(BF)], axis=1
        )
        nxt = g * coef_ref[t, 0] + dot_nt(dgs, wh_ref[...])
        gate_ref[t, :, :width] = an.astype(BF)
        gate_ref[t, :, width:] = dgs
        store(t).start()
        db_ref[:, :width] += fold(az)
        db_ref[:, width : 2 * width] += fold(ar)
        db_ref[:, 2 * width :] += fold(an)
        return nxt

    g = lax.fori_loop(0, hops, step, pgrad_ref[...].astype(F32), unroll=4)
    pathgrad_ref[...] = g
    wx = jnp.concatenate([wx_ref[:, 2 * width :], wx_ref[:, : 2 * width]], axis=1)
    per = 4
    for t in range(0, hops, per):
        rows = gate_ref[t : t + per, :, : 3 * width].reshape(per * flows, 3 * width)
        dx_ref[t * flows : (t + per) * flows, :] = dot_nt(rows, wx).astype(BF)
    for copy in sum_slots(row_ref, dx_ref[...], part_ref, part_hbm, sem_part):
        copy.wait()
    for t in range(hops):
        store(t).wait()


def weight_kernel(
    place_ref, x_ref, prior_ref, gate_ref, db_ref, mlp_ref,
    mine_ref, other_ref, pack_ref, awx_ref, awh_ref,
):
    per, flows, width = x_ref.shape
    i = pl.program_id(0)
    rows = per * flows
    gates = gate_ref[...].reshape(rows, 4 * width)
    gx = dot_tn(x_ref[...].reshape(rows, width), gates[:, : 3 * width])
    gh = dot_tn(prior_ref[...].reshape(rows, width), gates[:, width:])

    @pl.when(i == 0)
    def _():
        awx_ref[...] = gx
        awh_ref[...] = gh

    @pl.when(i > 0)
    def _():
        awx_ref[...] += gx
        awh_ref[...] += gh

    @pl.when(i == pl.num_programs(0) - 1)
    def _():
        for k in range(3):
            s = slice(k * width, (k + 1) * width)
            to = (k + 2) % 3
            pack_ref[to * width : (to + 1) * width, :] = awx_ref[:, s].astype(BF)
            pack_ref[(3 + k) * width : (4 + k) * width, :] = awh_ref[:, s].astype(BF)
        base = 9 * width
        pack_ref[6 * width : base + 16, :] = mlp_ref[...]
        b = jnp.sum(db_ref[...], axis=0, keepdims=True)
        tail = jnp.concatenate(
            [b[:, k * width : (k + 1) * width] for k in range(3)] + [jnp.zeros((13, width), F32)],
            axis=0,
        )
        pack_ref[base + 16 : base + 32, :] = tail.astype(BF)
        rest = pack_ref.shape[0] - base - 32
        pack_ref[base + 32 :, :] = jnp.zeros((rest, width), BF)
        half = mine_ref.shape[0]
        core = place_ref[1]
        mine_ref[...] = pack_ref[pl.ds(pl.multiple_of(core * half, 256), half), :]
        other_ref[...] = pack_ref[pl.ds(pl.multiple_of((1 - core) * half, 256), half), :]


def finish_kernel(got_ref, srow_ref, direct_ref, out_ref):
    links = direct_ref.shape[0]
    sel = jnp.concatenate(
        [pick_rows(srow_ref[k : k + 1, :], links) for k in range(srow_ref.shape[0])], axis=1
    )
    out_ref[...] = direct_ref[...] + dot(sel, got_ref[...])


def swap(blocks, axes=OL, groups=None):
    return lax.all_to_all(
        blocks, axes, split_axis=0, concat_axis=0, tiled=True, axis_index_groups=groups
    )


def swap_named(rows, group):
    return swap(rows.reshape(group, -1, rows.shape[1])).reshape(rows.shape)


def total(v):
    return jnp.sum(v.astype(F32), axis=0).astype(BF)


def pair_kernel(place_ref, pack_ref, got_ref, *out_refs):
    x = place_ref[0]
    chips = len(out_refs)
    part = out_refs[0].shape[0]
    for k in range(chips):
        rows = pl.ds(pl.multiple_of(lax.rem(x + k, chips) * part, 64), part)
        both = pack_ref[rows, :].astype(F32) + got_ref[rows, :].astype(F32)
        out_refs[k][...] = both.astype(BF)


def ring_sum_kernel(place_ref, *refs):
    count = len(refs) // 2
    rows = refs[count].shape[0]
    for k in range(count):
        at = pl.ds(pl.multiple_of(lax.rem(place_ref[2] + k, count) * rows, 16), rows)
        value = refs[0][at, :].astype(F32)
        for ref in refs[1:count]:
            value = value + ref[at, :].astype(F32)
        refs[count + k][...] = value.astype(BF)


def outer_join_kernel(place_ref, *refs):
    out_ref = refs[-1]
    count = len(refs) - 1
    rows = refs[0].shape[0]
    for k in range(count):
        to = lax.rem(place_ref[2] - k + count, count)
        out_ref[pl.ds(pl.multiple_of(to * rows, 16), rows), :] = refs[k][...]


def around(piece, axis):
    count = lax.axis_size(axis)
    got = [piece]
    for k in range(1, count):
        got.append(lax.ppermute(piece, axis, [(i, (i + k) % count) for i in range(count)]))
    return got


def unpack_kernel(place_ref, *refs, scale):
    x = place_ref[0]
    core = place_ref[1]
    chips = (len(refs) - 8) // 2
    mine = refs[:chips]
    got = refs[chips : 2 * chips]
    wx_ref, wh_ref, bias_ref, w1_ref, b1_ref, w2_ref, b2_ref, all_ref = refs[2 * chips :]
    rows, width = mine[0].shape
    for k in range(chips):
        c = lax.rem(x - k + chips, chips)
        all_ref[pl.ds(pl.multiple_of((core * chips + c) * rows, 64), rows), :] = mine[k][...]
        all_ref[pl.ds(pl.multiple_of(((1 - core) * chips + c) * rows, 64), rows), :] = got[k][...]
    take = lambda a, n: all_ref[a : a + n, :].astype(F32) * scale
    for k in range(3):
        s = slice(k * width, (k + 1) * width)
        wx_ref[:, s] = take(k * width, width)
        wh_ref[:, s] = take((3 + k) * width, width)
    w1_ref[...] = take(6 * width, 2 * width)
    w2_ref[...] = take(8 * width, width)
    tail = take(9 * width, 32)
    b1_ref[...] = tail[0:1]
    b2_ref[...] = tail[1:2]
    for k in range(3):
        bias_ref[k * width : (k + 1) * width] = tail[16 + k]


def whereabouts():
    rep = lax.axis_index("replica")
    spots = [rep // 2, rep % 2, lax.axis_index("outer"), lax.axis_index("link")]
    return jnp.stack(spots).astype(jnp.int32)


def sum_everywhere(mine, other, place, scale):
    rows, width = mine.shape
    rows = 2 * rows
    reps = lax.axis_size("replica")
    chips = reps // 2
    part = rows // reps
    pairs = [(i, i ^ 1) for i in range(reps)]
    ahead = [[(i, (i + 2 * k) % reps) for i in range(reps)] for k in range(chips)]
    smem = pl.BlockSpec(memory_space=pltpu.SMEM)
    vmem = pl.BlockSpec(memory_space=pltpu.VMEM)
    got = lax.ppermute(other, "replica", pairs)
    mine = call(
        pair_kernel, (sds((part, width), BF),) * chips, in_specs=[smem, vmem, vmem]
    )(place, mine, got)
    got = [lax.ppermute(mine[k], "replica", ahead[k]) for k in range(1, chips)]
    lines = lax.axis_size("outer")
    mine = call(
        ring_sum_kernel,
        (sds((part // lines, width), BF),) * lines,
        in_specs=[smem] + [vmem] * chips,
    )(place, mine[0], *got)
    got = []
    for k in range(1, lines):
        hops = [(i, (i + k) % lines) for i in range(lines)]
        got.append(lax.ppermute(mine[k], "outer", hops))
    mine = sum((g.astype(F32) for g in got), mine[0].astype(F32)).astype(BF)
    count = lax.axis_size("link")
    mine = total(swap(jnp.broadcast_to(mine[None], (count,) + mine.shape), "link"))
    got = around(mine, "outer")
    mine = call(
        outer_join_kernel, sds((part, width), BF), in_specs=[smem] + [vmem] * len(got)
    )(place, *got)
    whole = [mine]
    for k in range(1, chips):
        whole.append(lax.ppermute(mine, "replica", ahead[k]))
    mine = whole
    got = [lax.ppermute(m, "replica", pairs) for m in mine]
    return call(
        lambda *refs: unpack_kernel(*refs, scale=scale),
        (
            sds((width, 3 * width), F32),
            sds((width, 3 * width), F32),
            sds((3 * width,), F32),
            sds((2 * width, width), F32),
            sds((1, width), F32),
            sds((width, width), F32),
            sds((1, width), F32),
        ),
        in_specs=[smem] + [vmem] * (2 * chips),
        scratch_shapes=[pltpu.VMEM((rows, width), BF)],
    )(place, *mine, *got)


def body(
    link_in, path_in, hop_slots, hop_lens, failed, serve_index, link_grad, path_grad,
    gru_wx, gru_wh, gru_bias, mlp_w1, mlp_b1, mlp_w2, mlp_b2,
):
    link_rows = link_in[0]
    links, width = link_rows.shape
    serve_rows = serve_index[0, :, 0, :]
    group, cap = serve_rows.shape
    slots = group * cap
    serve_row = serve_rows.reshape(slots // 128, 128)
    flows, hops = hop_slots.shape[1:]
    lens_col = hop_lens[0][:, None]
    slot_col = jnp.where(jnp.arange(hops, dtype=jnp.int32)[None, :] < lens_col, hop_slots[0], -1)
    slot_row = slot_col.T
    keep = (1 - failed[0]).astype(F32)[:, None]
    bias = gru_bias[None]
    wide = 3 * width

    vmem = pl.BlockSpec(memory_space=pltpu.VMEM)
    smem = pl.BlockSpec(memory_space=pltpu.SMEM)
    hbm = pl.BlockSpec(memory_space=pltpu.HBM)
    blocks = group // 8
    rows_out = [pltpu.VMEM((slots, width), BF)]
    sent = call(
        serve_kernel,
        sds((slots, width), BF),
        out_specs=hbm,
        scratch_shapes=rows_out + [pltpu.SemaphoreType.DMA((blocks,))],
    )(link_rows, serve_rows)
    fetched = swap_named(sent, group)
    place = whereabouts()
    x, states, priors, part, path_out = call(
        forward_kernel,
        (
            sds((hops, flows, width), BF),
            sds((hops, flows, width), F32),
            sds((hops, flows, width), BF),
            sds((slots, width), BF),
            sds((flows, width), BF),
        ),
        mib=62,
        out_specs=[hbm] * 4 + [vmem],
        scratch_shapes=[
            pltpu.VMEM((hops, flows, width), BF),
            pltpu.VMEM((hops, flows, width), F32),
            pltpu.VMEM((hops, flows, width), BF),
            pltpu.VMEM((hops, flows, wide), F32),
            pltpu.VMEM((hops, flows, width), BF),
            *rows_out,
            pltpu.SemaphoreType.DMA((3,)),
            pltpu.SemaphoreType.DMA((slots // 512,)),
        ],
    )(fetched, slot_col, slot_row, lens_col, path_in[0], gru_wx, gru_wh, bias)
    arrived = swap_named(part, group)

    per = 4
    steps = lambda *tail: pl.BlockSpec((per,) + tail, lambda i: (i,) + (0,) * len(tail))
    whole = lambda *shape: pl.BlockSpec(shape, lambda i: (0,) * len(shape))
    coef = call(
        coef_kernel,
        sds((hops, 5, flows, width), F32),
        mib=58,
        grid=(hops // per,),
        in_specs=[
            steps(flows, width),
            steps(flows, width),
            whole(flows, 1),
            whole(width, wide),
            whole(width, wide),
            whole(1, wide),
        ],
        out_specs=steps(5, flows, width),
    )(x, states, lens_col, gru_wx, gru_wh, bias)

    sent, mids, db1 = call(
        link_kernel,
        (
            sds((slots, width), BF),
            sds((3 * links, width), BF),
            sds((1, width), F32),
        ),
        mib=62,
        out_specs=[hbm, hbm, vmem],
        scratch_shapes=rows_out
        + [
            pltpu.VMEM((3 * links, width), BF),
            pltpu.SemaphoreType.DMA((1,)),
            pltpu.SemaphoreType.DMA((blocks,)),
        ],
    )(arrived, serve_row, serve_rows, link_rows, link_grad[0], keep, mlp_w1, mlp_b1[None], mlp_w2)
    returned = swap_named(sent, group)
    link_out, direct, mlp_pack = call(
        link_rest_kernel,
        (
            sds((links, width), BF),
            sds((links, width), F32),
            sds((3 * width + 16, width), BF),
        ),
        mib=58,
    )(link_rows, link_grad[0], keep, mids, db1, mlp_w1, mlp_w2, mlp_b2[None])

    dpart, path_back, gates, db = call(
        backward_kernel,
        (
            sds((slots, width), BF),
            sds((flows, width), F32),
            sds((hops, flows, 4 * width), BF),
            sds((8, wide), F32),
        ),
        mib=51,
        in_specs=[vmem] * 6 + [hbm],
        out_specs=[hbm, vmem, hbm, vmem],
        scratch_shapes=[
            pltpu.VMEM((hops, flows, width), BF),
            pltpu.VMEM((hops, 5, flows, width), F32),
            pltpu.VMEM((hops, flows, 4 * width), BF),
            pltpu.VMEM((hops * flows, width), BF),
            *rows_out,
            pltpu.SemaphoreType.DMA((hops,)),
            pltpu.SemaphoreType.DMA((hops,)),
            pltpu.SemaphoreType.DMA((slots // 512,)),
        ],
    )(returned, slot_col, slot_row, path_grad[0], gru_wx, gru_wh, coef)
    owned = swap_named(dpart, group)

    mine, other = call(
        weight_kernel,
        (sds((5 * width, width), BF),) * 2,
        mib=58,
        grid=(hops // per,),
        in_specs=[
            smem,
            steps(flows, width),
            steps(flows, width),
            steps(flows, 4 * width),
            whole(8, wide),
            whole(3 * width + 16, width),
        ],
        out_specs=[whole(5 * width, width)] * 2,
        scratch_shapes=[
            pltpu.VMEM((10 * width, width), BF),
            pltpu.VMEM((width, wide), F32),
            pltpu.VMEM((width, wide), F32),
        ],
    )(place, x, priors, gates, db, mlp_pack)
    link_back = call(finish_kernel, sds((links, width), F32), mib=58)(owned, serve_row, direct)

    count = lax.axis_size("replica") * lax.axis_size("outer") * lax.axis_size("link")
    scale = float(count * links) ** (-0.5)
    wx, wh, bias, w1, b1, w2, b2 = sum_everywhere(mine, other, place, scale)
    return (
        link_out[None],
        path_out[None],
        link_back[None],
        path_back[None],
        wx,
        wh,
        bias,
        w1,
        b1.reshape(width),
        w2,
        b2.reshape(width),
    )


def solution(mesh):
    over = P("replica", OL, None)
    flat = P("replica", OL)

    return jax.shard_map(
        body,
        mesh=mesh,
        in_specs=(
            over, over, over, flat, flat, P("replica", None, OL, None), over, over,
            P(), P(), P(), P(), P(), P(), P(),
        ),
        out_specs=(over, over, over, over, P(), P(), P(), P(), P(), P(), P()),
        check_vma=False,
    )
```
